32 devices in a mesh: weld: 8 (over y, x, core), trans: 4 (over z).
Axes of the slice: x: 2, y: 2, z: 4, core: 2. Of those that a mesh axis runs over, the one named last changes fastest.
Arguments:
- features: bfloat16 [64, 128, 16, 128], P('weld', 'trans'), as said below
- pair_offsets: int32 [64, 128, 12], P('weld', 'trans'), may hold values from 0 to 8
- pair_kernel: int32 [64, 128, 12], P('weld', 'trans'), may hold values from 0 to 15
- kernels: bfloat16 [16, 128, 128], replicated
- send_list: int32 [8, 4, 4, 32], P('weld', 'trans'), may hold values from 0 to 256, as said below
- wall_slots: int32 [8, 4, 16, 16], P('weld', 'trans'), may hold values from 0 to 128, as said below
- wall_kernel: int32 [8, 4, 16, 16], P('weld', 'trans'), may hold values from 0 to 7
- wall_kernels: bfloat16 [8, 128, 128], replicated, as said below
Outputs:
- rates: bfloat16 [64, 128, 16, 128], P('weld', 'trans')
- walls: bfloat16 [8, 4, 16, 16, 128], P('weld', 'trans')
The draws below stay inside these ranges and needn't reach their ends.
Inputs may be any that keep to these rules, and one draw needn't show every extreme that they name: `send_list`: A value of 256 marks an empty slot; on each device one wall owner gets all 32 slots and every other owner gets fewer. `wall_slots`: A value of 128 reads the zero tile. `features`: channel 0 is positive. `wall_kernels`: entries are non-negative.
All inputs are finite; a program needn't handle non-finite values.
Results may differ from the reference program's by a relative error of at most 0.0075.
Values may be sent and summed in bfloat16 or wider, within the bound.
No kernel may reach another device: no remote copies, remote signals or barrier semaphores. Data moves between devices by JAX's collectives and lax.ppermute only.
A program may use at most 64 MiB of HBM per device.

```python
import jax
import jax.numpy as jnp
from jax import lax

GW = 8
GT = 32
F = 16
TILE = 128
NB = 12
KB = 16
KW = 8
CAP = 32
WT = 16
NW = 16
SLABS = 8
PEERS = 4
NWT = 64
NTT = 128


def draw_features(key, part):
    first, second = jax.random.split(key, 2)
    volume = jnp.exp(jax.random.uniform(first, (NWT, NTT, 1, TILE), jnp.float32, -0.693, 0.693))
    rest = jax.random.normal(second, (NWT, NTT, F - 1, TILE), jnp.float32)
    return jnp.concatenate([volume, rest], axis=2).astype(jnp.bfloat16)


def draw_kernels(key, part):
    eye = jnp.eye(TILE, dtype=jnp.float32)[None]
    noise = jax.random.normal(key, (KB, TILE, TILE), jnp.float32)
    return (noise * (TILE * NB) ** (-0.5) + eye * 2.0 * NB ** (-0.5)).astype(jnp.bfloat16)


def draw_wall_kernels(key, part):
    eye = jnp.eye(TILE, dtype=jnp.float32)[None]
    noise = jax.random.uniform(key, (KW, TILE, TILE), jnp.float32, 0.0, 2.0)
    return (noise / (TILE * NW) + eye / NW).astype(jnp.bfloat16)


def draw_send_list(key, part):
    first, second, third = jax.random.split(key, 3)
    counts = jax.random.randint(first, (SLABS, PEERS, PEERS), 1, CAP)
    full = jax.random.randint(second, (SLABS, PEERS, 1), 0, PEERS)
    owners = jnp.arange(PEERS, dtype=jnp.int32)[None, None, :]
    counts = jnp.where(owners == full, CAP, counts)
    picks = jax.random.randint(third, (SLABS, PEERS, PEERS, CAP), 0, GW * GT)
    slots = jnp.arange(CAP, dtype=jnp.int32)[None, None, None, :]
    return jnp.where(slots < counts[..., None], picks, GW * GT).astype(jnp.int32)


def draw_wall_slots(key, part):
    first, second = jax.random.split(key)
    inner = jax.random.randint(first, (SLABS, PEERS, WT, 1), 1, NW // 2 + 1)
    position = jnp.arange(PEERS, dtype=jnp.int32)[None, :, None, None]
    clamp = (position == 0) | (position == PEERS - 1)
    live = jnp.where(clamp, NW, inner)
    picks = jax.random.randint(second, (SLABS, PEERS, WT, NW), 0, PEERS * CAP)
    entries = jnp.arange(NW, dtype=jnp.int32)[None, None, None, :]
    return jnp.where(entries < live, picks, PEERS * CAP).astype(jnp.int32)


def plant(result, own_key, least, largest):
    shape = result.shape
    index_at = [jax.random.randint(jax.random.fold_in(own_key, axis), (), 0, shape[axis]) for axis in range(len(shape))]
    result = result.at[tuple(index_at)].set(least)
    longest = shape.index(max(shape))
    index_at[longest] = (index_at[longest] + 1) % shape[longest]
    return result.at[tuple(index_at)].set(largest)


def setup_inputs(seed: int = 0) -> dict:
    splits = jax.random.split(jax.random.key(seed), 9)
    features = draw_features(jax.random.fold_in(splits[8], 71), 0)
    pair_offsets = plant(jax.random.randint(splits[1], (NWT, NTT, NB), 0, 9), jax.random.fold_in(splits[1], 1), 0, 8).astype(jnp.int32)
    pair_kernel = plant(jax.random.randint(splits[2], (NWT, NTT, NB), 0, KB), jax.random.fold_in(splits[2], 1), 0, KB - 1).astype(jnp.int32)
    kernels = draw_kernels(jax.random.fold_in(splits[8], 71), 0)
    send_list = draw_send_list(jax.random.fold_in(splits[8], 71), 0)
    wall_slots = draw_wall_slots(jax.random.fold_in(splits[8], 71), 0)
    wall_kernel = plant(jax.random.randint(splits[6], (SLABS, PEERS, WT, NW), 0, KW), jax.random.fold_in(splits[6], 1), 0, KW - 1).astype(jnp.int32)
    wall_kernels = draw_wall_kernels(jax.random.fold_in(splits[8], 71), 0)
    return {"features": features, "pair_offsets": pair_offsets, "pair_kernel": pair_kernel, "kernels": kernels, "send_list": send_list, "wall_slots": wall_slots, "wall_kernel": wall_kernel, "wall_kernels": wall_kernels}


def tile_terms(gathered, kinds, bank):
    chosen = bank[kinds].astype(jnp.float32)
    return jnp.einsum("nbfp,nbpq->nfq", gathered.astype(jnp.float32), chosen, precision=lax.Precision.HIGHEST)


def reference(features, pair_offsets, pair_kernel, kernels, send_list, wall_slots, wall_kernel, wall_kernels):
    padded = jnp.pad(features, ((1, 1), (1, 1), (0, 0), (0, 0)))
    width = NTT + 2
    flat = padded.reshape(-1, F, TILE)
    columns = jnp.arange(NTT, dtype=jnp.int32)

    def row_rates(args):
        row, offsets, kinds = args
        index = (row + offsets // 3) * width + columns[:, None] + offsets % 3
        gathered = flat[index]
        return tile_terms(gathered, kinds, kernels).astype(jnp.bfloat16)

    rates = lax.map(row_rates, (jnp.arange(NWT, dtype=jnp.int32), pair_offsets, pair_kernel))

    local = features.reshape(SLABS, GW, PEERS, GT, F, TILE).transpose(0, 2, 1, 3, 4, 5)
    local = local.reshape(SLABS, PEERS, GW * GT, F, TILE)
    extended = jnp.concatenate([local, jnp.zeros((SLABS, PEERS, 1, F, TILE), jnp.bfloat16)], axis=2)
    sources = jnp.arange(PEERS, dtype=jnp.int32)[:, None, None]

    def slab_walls(args):
        ext_slab, sends, slots, kinds = args
        buffers = ext_slab[sources, sends]
        received = buffers.transpose(1, 0, 2, 3, 4).reshape(PEERS, PEERS * CAP, F, TILE)
        received = jnp.concatenate([received, jnp.zeros((PEERS, 1, F, TILE), jnp.bfloat16)], axis=1)

        def owner(inner):
            got, slot_ids, kind_ids = inner
            sums = tile_terms(got[slot_ids], kind_ids, wall_kernels)
            return (sums / (1.0 + sums[:, 0:1, :])).astype(jnp.bfloat16)

        return lax.map(owner, (received, slots, kinds))

    walls = lax.map(slab_walls, (extended, send_list, wall_slots, wall_kernel))
    return (rates, walls)
```

```python
import functools

import jax
import jax.numpy as jnp
from jax import lax
from jax.experimental import pallas as pl
from jax.experimental.pallas import tpu as pltpu
from jax.sharding import PartitionSpec as P

SMEM = pl.BlockSpec(memory_space=pltpu.SMEM)
VMEM = pl.BlockSpec(memory_space=pltpu.VMEM)
ANY = pl.BlockSpec(memory_space=pl.ANY)
MIB = 1 << 20


def pick(cond, a, b):
    return lax.select(cond, jnp.int32(a), jnp.int32(b))


def index_kernel(dims, off_ref, kind_ref, slot_ref, wkind_ref, local_ref, halo_ref, wall_ref):
    gw, gt, bank, wall_bank, peers, cap = dims
    w, t = lax.axis_index("weld"), lax.axis_index("trans")
    off, kind = off_ref[...], kind_ref[...]
    dr = (off * 11) >> 5
    row = lax.broadcasted_iota(jnp.int32, off.shape, 1) + dr - 1
    col = lax.broadcasted_iota(jnp.int32, off.shape, 2) + (off - 3 * dr) - 1
    above, below = row < 0, row >= gw
    left, right = col < 0, col >= gt
    side = left | right
    inside = ~(above | below | side)
    local = jnp.where(inside, kind * (gw * gt) + row * gt + col, bank * gw * gt)
    even_w, even_t = lax.rem(w, 2) == 0, lax.rem(t, 2) == 0
    base_m, base_p = pick(even_w, gt, 0), pick(even_w, 0, gt)
    base_l = pick(even_t, 2 * gt + gw + 2, 2 * gt)
    base_r = pick(even_t, 2 * gt, 2 * gt + gw + 2)
    size = 2 * gt + 2 * gw + 4
    place = jnp.where(
        left,
        base_l + row + 1,
        jnp.where(right, base_r + row + 1, jnp.where(above, base_m + col, base_p + col)),
    )
    outside = (left & (t == 0)) | (right & (t == peers - 1))
    halo = jnp.where(inside | outside, bank * size, kind * size + place)
    local_ref[:, :, :gt] = local
    halo_ref[:, :, :gt] = halo
    slot = slot_ref[...]
    sender = slot // cap
    wall_ref[...] = jnp.where(
        slot >= peers * cap,
        wall_bank * peers * cap,
        wkind_ref[...] * (peers * cap) + (sender ^ t) * cap + (slot - sender * cap),
    )


def outgoing_kernel(dims, merged, x_ref, near_ref, far_ref, list_ref, *outs):
    gw, gt, peers, cap = dims
    w, t = lax.axis_index("weld"), lax.axis_index("trans")
    empty = jnp.zeros(x_ref.shape[1:], x_ref.dtype)
    for k in range(peers):
        owner = t ^ k

        def body(c, _, owner=owner, k=k):
            item = list_ref[owner, c]
            tile = x_ref[jnp.minimum(item, gw * gt - 1)]
            outs[k][c] = jnp.where(item < gw * gt, tile, empty)
            return 0

        lax.fori_loop(0, cap, body, 0, unroll=8)
    even_w, even_t = lax.rem(w, 2) == 0, lax.rem(t, 2) == 0
    for which, ref in enumerate(merged):
        base = cap if len(outs) == peers else 0
        column = pick(even_t, gt - 1, 0) if which == 0 else pick(even_t, 0, gt - 1)
        a, b = near_ref[column], far_ref[column]
        outs[ref][base] = jnp.where(even_w, b, a)
        outs[ref][base + gw + 1] = jnp.where(even_w, a, b)
        for r in range(gw):
            outs[ref][base + 1 + r] = x_ref[r * gt + column]


def tree(terms):
    while len(terms) > 1:
        terms = [sum(terms[i : i + 2][1:], terms[i]) for i in range(0, len(terms), 2)]
    return terms[0]


def products(rows, bank_ref, table_ref, step):
    tiles = rows.shape[0] // 16
    for j in range(0, bank_ref.shape[0], 2):
        both = jnp.concatenate([bank_ref[j], bank_ref[j + 1]], axis=1)
        wide = jnp.dot(rows, both, preferred_element_type=jnp.float32).astype(table_ref.dtype)
        for h in range(2):
            start = (j + h) * step
            part = wide[:, 128 * h : 128 * (h + 1)]
            table_ref[start : start + tiles] = part.reshape(tiles, 16, 128)


def local_kernel(dims, index_ref, x_ref, bank_ref, out_ref, table_ref):
    gw, gt, entries = dims
    tiles = gw * gt
    table_ref[table_ref.shape[0] - 1] = jnp.zeros(table_ref.shape[1:], table_ref.dtype)
    products(x_ref[...].reshape(tiles * 16, 128), bank_ref, table_ref, tiles)

    def body(r, _):
        for c in range(gt):
            terms = [
                table_ref[index_ref[n * gw + r, c]].astype(jnp.float32) for n in range(entries)
            ]
            out_ref[r * gt + c] = tree(terms).astype(out_ref.dtype)
        return 0

    lax.fori_loop(0, gw, body, 0)


def finish_kernel(dims, index_ref, wall_index_ref, *refs):
    gw, gt, entries, peers, cap, walls = dims
    near_ref, far_ref, own_ref = refs[:3]
    merged = peers == 4
    count = peers - 1 + (0 if merged else 2)
    got = refs[3 : 3 + count]
    bank_ref, wall_bank_ref, _, rates_ref, walls_ref = refs[3 + count : 8 + count]
    table_ref, wall_table_ref, rows_ref, cols_ref, in_sem, out_sem = refs[8 + count :]

    def edges(to_hbm):
        pairs = []
        for e, r in enumerate((0, gw - 1)):
            pairs.append((rates_ref.at[r], rows_ref.at[e]))
        for e, c in enumerate((0, gt - 1)):
            pairs.append((rates_ref.at[1 : gw - 1, c], cols_ref.at[e]))
        return [
            pltpu.make_async_copy(b, a, out_sem.at[i])
            if to_hbm
            else pltpu.make_async_copy(a, b, in_sem.at[i])
            for i, (a, b) in enumerate(pairs)
        ]

    fetch = edges(False)
    for copy in fetch:
        copy.start()
    depth = gw + 2
    size = 2 * gt + 2 * depth
    if merged:
        col_a, col_b = got[0][cap : cap + depth], got[2][cap : cap + depth]
    else:
        col_a, col_b = got[-2][...], got[-1][...]
    ring = jnp.concatenate([near_ref[...], far_ref[...], col_a, col_b], axis=0)
    blank = jnp.zeros(table_ref.shape[1:], table_ref.dtype)
    table_ref[table_ref.shape[0] - 1] = blank
    products(ring.reshape(size * 16, 128), bank_ref, table_ref, size)
    wall_table_ref[wall_table_ref.shape[0] - 1] = blank
    received = jnp.concatenate([own_ref[...]] + [g[:cap] for g in got[: peers - 1]], axis=0)
    products(received.reshape(peers * cap * 16, 128), wall_bank_ref, wall_table_ref, peers * cap)
    for copy in fetch:
        copy.wait()

    def extra(r, c):
        return tree(
            [table_ref[index_ref[n * gw + r, c]].astype(jnp.float32) for n in range(entries)]
        )

    def row_body(e, _):
        for c in range(gt):
            base = rows_ref[e, c].astype(jnp.float32)
            rows_ref[e, c] = (base + extra(e * (gw - 1), c)).astype(rows_ref.dtype)
        return 0

    lax.fori_loop(0, 2, row_body, 0)

    for e, c in enumerate((0, gt - 1)):

        def col_body(r, _, e=e, c=c):
            base = cols_ref[e, r].astype(jnp.float32)
            cols_ref[e, r] = (base + extra(r + 1, c)).astype(cols_ref.dtype)
            return 0

        lax.fori_loop(0, gw - 2, col_body, 0)
    store = edges(True)
    for copy in store:
        copy.start()

    def wall_body(j, _):
        picked = [
            wall_table_ref[wall_index_ref[j, m]].astype(jnp.float32)
            for m in range(wall_index_ref.shape[1])
        ]
        sums = tree(picked)
        walls_ref[j] = (sums / (1.0 + sums[0:1, :])).astype(walls_ref.dtype)
        return 0

    lax.fori_loop(0, walls, wall_body, 0)
    for copy in store:
        copy.wait()


def pairing(count, shift):
    pairs = []
    for low in range(shift, count - 1, 2):
        pairs += [(low, low + 1), (low + 1, low)]
    return pairs


def on_device(
    features, pair_offsets, pair_kernel, kernels, send_list, wall_slots, wall_kernel, wall_kernels
):
    gw, gt, channels, tile = features.shape
    entries = pair_offsets.shape[2]
    bank, wall_bank = kernels.shape[0], wall_kernels.shape[0]
    peers, cap = send_list.shape[2:]
    walls, picks = wall_slots.shape[2:]
    weld = lax.axis_size("weld")
    merged = peers == 4
    depth = gw + 2
    size = 2 * gt + 2 * depth
    i32, bf16 = jnp.int32, jnp.bfloat16
    tiles = features.reshape(gw * gt, channels, tile)

    even_w = lax.rem(lax.axis_index("weld"), 2) == 0
    low, high = pick(even_w, 0, gw - 1), pick(even_w, gw - 1, 0)
    near = lax.ppermute(
        lax.dynamic_index_in_dim(features, high, 0, False), "weld", pairing(weld, 0)
    )
    far = lax.ppermute(lax.dynamic_index_in_dim(features, low, 0, False), "weld", pairing(weld, 1))

    local_index, halo_index, wall_index = pl.pallas_call(
        functools.partial(index_kernel, (gw, gt, bank, wall_bank, peers, cap)),
        name="pair_index",
        out_shape=(
            jax.ShapeDtypeStruct((entries, gw, 128), i32),
            jax.ShapeDtypeStruct((entries, gw, 128), i32),
            jax.ShapeDtypeStruct((walls, picks), i32),
        ),
        in_specs=[VMEM] * 4,
        out_specs=(VMEM, VMEM, VMEM),
        cost_estimate=pl.CostEstimate(flops=400_000, bytes_accessed=300_000, transcendentals=0),
    )(
        pair_offsets.transpose(2, 0, 1),
        pair_kernel.transpose(2, 0, 1),
        wall_slots.reshape(walls, picks),
        wall_kernel.reshape(walls, picks),
    )
    local_index = local_index.reshape(entries * gw, 128)
    halo_index = halo_index.reshape(entries * gw, 128)

    lengths = [cap + (depth if merged and k in (1, 3) else 0) for k in range(peers)]
    if not merged:
        lengths += [depth, depth]
    sends = pl.pallas_call(
        functools.partial(
            outgoing_kernel, (gw, gt, peers, cap), (1, 3) if merged else (peers, peers + 1)
        ),
        name="outgoing",
        out_shape=tuple(jax.ShapeDtypeStruct((n, channels, tile), bf16) for n in lengths),
        in_specs=[VMEM, VMEM, VMEM, SMEM],
        out_specs=(VMEM,) * len(lengths),
        cost_estimate=pl.CostEstimate(flops=0, bytes_accessed=2 * MIB, transcendentals=0),
    )(tiles, near, far, send_list.reshape(peers, cap))
    got = [
        lax.ppermute(sends[k], "trans", [(i, i ^ k) for i in range(peers)])
        for k in range(1, peers)
    ]
    if not merged:
        got += [lax.ppermute(sends[peers + s], "trans", pairing(peers, s)) for s in range(2)]

    rows = gw * gt * channels
    rates = pl.pallas_call(
        functools.partial(local_kernel, (gw, gt, entries)),
        name="local_pairs",
        out_shape=jax.ShapeDtypeStruct((gw * gt, channels, tile), bf16),
        in_specs=[SMEM, VMEM, VMEM],
        out_specs=VMEM,
        scratch_shapes=[pltpu.VMEM((bank * gw * gt + 1, channels, tile), bf16)],
        compiler_params=pltpu.CompilerParams(vmem_limit_bytes=40 * MIB),
        cost_estimate=pl.CostEstimate(
            flops=2 * rows * tile * tile * bank, bytes_accessed=30 * MIB, transcendentals=0
        ),
    )(local_index, tiles, kernels)

    count = len(got)
    rates, wall_out = pl.pallas_call(
        functools.partial(finish_kernel, (gw, gt, entries, peers, cap, walls)),
        name="halo_and_walls",
        out_shape=(
            jax.ShapeDtypeStruct((gw, gt, channels, tile), bf16),
            jax.ShapeDtypeStruct((walls, channels, tile), bf16),
        ),
        in_specs=[SMEM, SMEM] + [VMEM] * (5 + count) + [ANY],
        out_specs=(ANY, VMEM),
        scratch_shapes=[
            pltpu.VMEM((bank * size + 1, channels, tile), bf16),
            pltpu.VMEM((wall_bank * peers * cap + 1, channels, tile), bf16),
            pltpu.VMEM((2, gt, channels, tile), bf16),
            pltpu.VMEM((2, gw - 2, channels, tile), bf16),
            pltpu.SemaphoreType.DMA((4,)),
            pltpu.SemaphoreType.DMA((4,)),
        ],
        input_output_aliases={7 + count: 0},
        compiler_params=pltpu.CompilerParams(vmem_limit_bytes=48 * MIB),
        cost_estimate=pl.CostEstimate(
            flops=2 * size * channels * tile * tile * bank,
            bytes_accessed=8 * MIB,
            transcendentals=0,
        ),
    )(
        halo_index,
        wall_index,
        near,
        far,
        sends[0],
        *got,
        kernels,
        wall_kernels,
        rates.reshape(gw, gt, channels, tile),
    )
    return rates, wall_out.reshape(1, 1, walls, channels, tile)


def solution(mesh):
    in_specs = (
        P("weld", "trans", None, None),
        P("weld", "trans", None),
        P("weld", "trans", None),
        P(),
        P("weld", "trans", None, None),
        P("weld", "trans", None, None),
        P("weld", "trans", None, None),
        P(),
    )
    out_specs = (P("weld", "trans", None, None), P("weld", "trans", None, None, None))
    return jax.shard_map(
        on_device, mesh=mesh, in_specs=in_specs, out_specs=out_specs, check_vma=False
    )
```

```python
import functools

import jax
import jax.numpy as jnp
from jax import lax
from jax.experimental import pallas as pl
from jax.experimental.pallas import tpu as pltpu
from jax.sharding import PartitionSpec as P

SMEM = pl.BlockSpec(memory_space=pltpu.SMEM)
VMEM = pl.BlockSpec(memory_space=pltpu.VMEM)
HBM = pl.BlockSpec(memory_space=pl.ANY)
MIB = 1 << 20
UNROLLED = False


def pick(cond, a, b):
    return lax.select(cond, jnp.int32(a), jnp.int32(b))


def index_kernel(dims, off_ref, kind_ref, slot_ref, wkind_ref, local_ref, side_ref, wall_ref):
    gw, gt, bank, wall_bank, peers, cap = dims
    t = lax.axis_index("trans")
    off, kind = off_ref[...], kind_ref[...]
    dr = (off * 11) >> 5
    row = lax.broadcasted_iota(jnp.int32, off.shape, 1)
    band = row + dr - jnp.where(row < gw // 2, 0, gw // 2)
    col = lax.broadcasted_iota(jnp.int32, off.shape, 2) + (off - 3 * dr) - 1
    left, right = col < 0, col >= gt
    side = left | right
    rows = gw // 2 + 2
    local_ref[:, :, :gt] = jnp.where(
        side, bank * rows * gt, kind * (rows * gt) + band * gt + col
    )
    even_t = lax.rem(t, 2) == 0
    depth = gw + 2
    base = jnp.where(left, pick(even_t, depth, 0), pick(even_t, 0, depth))
    edge = (left & (t == 0)) | (right & (t == peers - 1))
    side_ref[:, :, :gt] = jnp.where(
        side & ~edge, kind * (2 * depth) + base + row + dr, bank * 2 * depth
    )
    slot = slot_ref[...]
    sender = slot // cap
    wall_ref[...] = jnp.where(
        slot >= peers * cap,
        wall_bank * peers * cap,
        wkind_ref[...] * (peers * cap) + (sender ^ t) * cap + (slot - sender * cap),
    )


def load_tiles(x_ref, held_ref, sem):
    count = x_ref.shape[0]
    return pltpu.make_async_copy(x_ref, held_ref.at[:count], sem)


def blank(ref):
    ref[ref.shape[0] - 1] = jnp.zeros(ref.shape[1:], ref.dtype)


def listed(held_ref, list_ref, owner, out_ref):
    for c in range(list_ref.shape[1]):
        out_ref[c] = held_ref[list_ref[owner, c]]


def first_kernel(dims, early, list_ref, x_ref, near_ref, far_ref, *refs):
    gw, gt = dims
    outs, (held_ref, sem) = refs[: len(early)], refs[len(early) :]
    w, t = lax.axis_index("weld"), lax.axis_index("trans")
    even = lax.rem(w, 2) == 0
    load = load_tiles(x_ref, held_ref, sem.at[0])
    load.start()
    rows = []
    for i, (ref, row) in enumerate(
        ((near_ref, pick(even, gw - 1, 0)), (far_ref, pick(even, 0, gw - 1)))
    ):
        rows.append(
            pltpu.make_async_copy(x_ref.at[pl.ds(row * gt, gt)], ref, sem.at[1 + i])
        )
        rows[i].start()
    blank(held_ref)
    load.wait()
    for k, ref in zip(early, outs):
        listed(held_ref, list_ref, t ^ k, ref)
    for copy in rows:
        copy.wait()


def second_kernel(dims, late, merged, list_ref, x_ref, near_ref, far_ref, *refs):
    gw, gt, cap = dims
    outs, (held_ref, sem, corner_sem) = refs[:-3], refs[-3:]
    w, t = lax.axis_index("weld"), lax.axis_index("trans")
    load = load_tiles(x_ref, held_ref, sem)
    load.start()
    blank(held_ref)
    corners, columns = [], []
    even_w, even_t = lax.rem(w, 2) == 0, lax.rem(t, 2) == 0
    for which in range(2):
        if merged:
            ref, base = outs[late.index((1, 3)[which])], cap
        else:
            ref, base = outs[len(late) + which], 0
        column = pick(even_t, gt - 1, 0) if which == 0 else pick(even_t, 0, gt - 1)
        for i, (corner, place) in enumerate(
            ((near_ref, pick(even_w, gw + 1, 0)), (far_ref, pick(even_w, 0, gw + 1)))
        ):
            copy = pltpu.make_async_copy(
                corner.at[column], ref.at[base + place], corner_sem.at[2 * which + i]
            )
            copy.start()
            corners.append(copy)
        columns.append((ref, base, column))
    load.wait()
    for ref, base, column in columns:
        for r in range(gw):
            ref[base + 1 + r] = held_ref[r * gt + column]
    for k, ref in zip(late, outs):
        listed(held_ref, list_ref, t ^ k, ref)
    for copy in corners:
        copy.wait()


def tree(terms):
    while len(terms) > 1:
        terms = [sum(terms[i : i + 2][1:], terms[i]) for i in range(0, len(terms), 2)]
    return terms[0]


def products(rows, bank_ref, j, targets):
    tiles = rows.shape[0] // 16
    both = jnp.concatenate([bank_ref[j], bank_ref[j + 1]], axis=1)
    wide = jnp.dot(rows, both, preferred_element_type=jnp.float32).astype(jnp.bfloat16)
    for h in range(2):
        part = wide[:, 128 * h : 128 * (h + 1)].reshape(tiles, 16, 128)
        for ref, step, at, low, count in targets:
            start = (j + h) * step + at
            ref[start : start + count] = part[low : low + count]


def local_kernel(dims, index_ref, x_ref, near_ref, far_ref, bank_ref, out_ref, *scratch):
    gw, gt, entries, unrolled = dims
    index, held, bank, top, low, total, sem = scratch
    even = lax.rem(lax.axis_index("weld"), 2) == 0
    half, kernels = gw // 2, bank.shape[0]
    step = (half + 2) * gt
    cut = (half + 1) * gt
    part = kernels // 2
    own = held.at[gt : (gw + 1) * gt]
    copies = [
        pltpu.make_async_copy(a, b, sem.at[i])
        for i, (a, b) in enumerate(
            (
                (bank_ref.at[:part], bank.at[:part]),
                (x_ref.at[:cut], own.at[:cut]),
                (near_ref, held.at[pl.ds(pick(even, (gw + 1) * gt, 0), gt)]),
                (far_ref, held.at[pl.ds(pick(even, 0, (gw + 1) * gt), gt)]),
                (bank_ref.at[part:], bank.at[part:]),
                (x_ref.at[cut:], own.at[cut:]),
                (index_ref, index),
            )
        )
    ]
    for copy in copies:
        copy.start()
    blank(top)
    blank(low)
    for copy in copies[:4]:
        copy.wait()

    def rows_of(first, count):
        return held[first * gt : (first + count) * gt].reshape(count * gt * 16, 128)

    def gather(table, r, c):
        terms = [table[index[n * gw + r, c]].astype(jnp.float32) for n in range(entries)]
        total[r * gt + c] = tree(terms).astype(total.dtype)

    upper = [(top, step, 0, 0, step), (low, step, 0, half * gt, 2 * gt)]
    lower = [(low, step, 2 * gt, 0, half * gt)]
    for j in range(0, kernels, 2):
        if j == part:
            copies[4].wait()
        products(rows_of(0, half + 2), bank, j, upper)
    copies[5].wait()
    copies[6].wait()
    cells = [(r, c) for r in range(half) for c in range(gt)]
    share = len(cells) * 2 // kernels
    for j in range(0, kernels, 2):
        products(rows_of(half + 2, half), bank, j, lower)
        if unrolled:
            for r, c in cells[j // 2 * share : (j // 2 + 1) * share]:
                gather(top, r, c)

    def store(first, count, i):
        span = pl.ds(first * gt, count * gt)
        copy = pltpu.make_async_copy(total.at[span], out_ref.at[span], sem.at[i])
        copy.start()
        return copy

    def body(r, _, table):
        for c in range(gt):
            gather(table, r, c)
        return 0

    if not unrolled:
        lax.fori_loop(0, half, functools.partial(body, table=top), 0)
    stores = [store(0, half, 0)]
    for i, first in enumerate(range(half, gw, half // 2)):
        if unrolled:
            for r in range(first, first + half // 2):
                body(r, 0, low)
        else:
            lax.fori_loop(first, first + half // 2, functools.partial(body, table=low), 0)
        stores.append(store(first, half // 2, 1 + i))
    for copy in stores:
        copy.wait()


def finish_kernel(dims, side_ref, wall_index_ref, *refs):
    gw, gt, entries, peers, cap, walls, merged = dims
    own_ref = refs[0]
    count = peers - 1 + (0 if merged else 2)
    got = refs[1 : 1 + count]
    bank_ref, wall_bank_ref, _, rates_ref, walls_ref = refs[1 + count : 6 + count]
    table_ref, wall_table_ref, cols_ref, in_sem, out_sem = refs[6 + count :]
    edges = [(rates_ref.at[:, c], cols_ref.at[e]) for e, c in enumerate((0, gt - 1))]
    fetch = [pltpu.make_async_copy(a, b, in_sem.at[e]) for e, (a, b) in enumerate(edges)]
    store = [pltpu.make_async_copy(b, a, out_sem.at[e]) for e, (a, b) in enumerate(edges)]
    for copy in fetch:
        copy.start()
    depth = gw + 2
    if merged:
        sides = [got[0][cap : cap + depth], got[2][cap : cap + depth]]
    else:
        sides = [got[-2][...], got[-1][...]]
    blank(table_ref)
    blank(wall_table_ref)
    ring = jnp.concatenate(sides, axis=0).reshape(2 * depth * 16, 128)
    for j in range(0, bank_ref.shape[0], 2):
        products(ring, bank_ref, j, [(table_ref, 2 * depth, 0, 0, 2 * depth)])
    slots = peers * cap
    received = jnp.concatenate([own_ref[...]] + [g[:cap] for g in got[: peers - 1]], axis=0)
    received = received.reshape(slots * 16, 128)
    for j in range(0, wall_bank_ref.shape[0], 2):
        products(received, wall_bank_ref, j, [(wall_table_ref, slots, 0, 0, slots)])
    for copy in fetch:
        copy.wait()
    for e, c in enumerate((0, gt - 1)):
        for r in range(gw):
            terms = [
                table_ref[side_ref[n * gw + r, c]].astype(jnp.float32) for n in range(entries)
            ]
            base = cols_ref[e, r].astype(jnp.float32)
            cols_ref[e, r] = (base + tree(terms)).astype(cols_ref.dtype)
        store[e].start()
    for j in range(walls):
        picked = [
            wall_table_ref[wall_index_ref[j, m]].astype(jnp.float32)
            for m in range(wall_index_ref.shape[1])
        ]
        sums = tree(picked)
        walls_ref[j] = (sums / (1.0 + sums[0:1, :])).astype(walls_ref.dtype)
    for copy in store:
        copy.wait()


def pairing(count, shift):
    pairs = []
    for low in range(shift, count - 1, 2):
        pairs += [(low, low + 1), (low + 1, low)]
    return pairs


def on_device(
    features, pair_offsets, pair_kernel, kernels, send_list, wall_slots, wall_kernel, wall_kernels
):
    gw, gt, channels, tile = features.shape
    entries = pair_offsets.shape[2]
    bank, wall_bank = kernels.shape[0], wall_kernels.shape[0]
    peers, cap = send_list.shape[2:]
    walls, picks = wall_slots.shape[2:]
    weld = lax.axis_size("weld")
    merged = peers == 4
    depth = gw + 2
    i32, bf16 = jnp.int32, jnp.bfloat16
    total = gw * gt
    tiles = features.reshape(total, channels, tile)
    lists = send_list.reshape(peers, cap)

    def stack(n):
        return jax.ShapeDtypeStruct((n, channels, tile), bf16)

    def buffer(n):
        return pltpu.VMEM((n, channels, tile), bf16)

    def cost(flops, mib):
        return pl.CostEstimate(flops=flops, bytes_accessed=mib * MIB, transcendentals=0)

    early = (2,) if merged else tuple(range(2, peers))
    late = (1, 3, 0) if merged else (1, 0)
    near_out, far_out, *early_out = pl.pallas_call(
        functools.partial(first_kernel, (gw, gt), early),
        name="edge_rows",
        out_shape=(stack(gt), stack(gt)) + (stack(cap),) * len(early),
        in_specs=[SMEM, HBM],
        out_specs=(HBM, HBM) + (VMEM,) * len(early),
        scratch_shapes=[buffer(total + 1), pltpu.SemaphoreType.DMA((3,))],
        cost_estimate=cost(0, 2),
    )(lists, tiles)
    near = lax.ppermute(near_out, "weld", pairing(weld, 0))
    far = lax.ppermute(far_out, "weld", pairing(weld, 1))
    got = {}
    for k, message in zip(early, early_out):
        got[k] = lax.ppermute(message, "trans", [(i, i ^ k) for i in range(peers)])

    table_index = jax.ShapeDtypeStruct((entries, gw, 128), i32)
    local_index, side_index, wall_index = pl.pallas_call(
        functools.partial(index_kernel, (gw, gt, bank, wall_bank, peers, cap)),
        name="pair_index",
        out_shape=(table_index, table_index, jax.ShapeDtypeStruct((walls, picks), i32)),
        in_specs=[VMEM] * 4,
        out_specs=(VMEM, VMEM, VMEM),
        cost_estimate=cost(1_000_000, 3),
    )(
        pair_offsets.transpose(2, 0, 1),
        pair_kernel.transpose(2, 0, 1),
        wall_slots.reshape(walls, picks),
        wall_kernel.reshape(walls, picks),
    )
    local_index = local_index.reshape(entries * gw, 128)
    side_index = side_index.reshape(entries * gw, 128)

    lengths = [cap + (depth if merged and k else 0) for k in late]
    if not merged:
        lengths += [depth, depth]
    late_out = pl.pallas_call(
        functools.partial(second_kernel, (gw, gt, cap), late, merged),
        name="edge_columns",
        out_shape=tuple(stack(n) for n in lengths),
        in_specs=[SMEM, HBM, HBM, HBM],
        out_specs=(VMEM,) * len(lengths),
        scratch_shapes=[
            buffer(total + 1),
            pltpu.SemaphoreType.DMA,
            pltpu.SemaphoreType.DMA((4,)),
        ],
        compiler_params=pltpu.CompilerParams(vmem_limit_bytes=8 * MIB),
        cost_estimate=cost(0, 2),
    )(lists, tiles, near, far)
    for k, message in zip(late, late_out):
        if k:
            got[k] = lax.ppermute(message, "trans", [(i, i ^ k) for i in range(peers)])
    own = late_out[late.index(0)]
    received = [got[k] for k in range(1, peers)]
    if not merged:
        received += [
            lax.ppermute(late_out[len(late) + s], "trans", pairing(peers, s)) for s in range(2)
        ]

    step = (gw // 2 + 2) * gt
    rates = pl.pallas_call(
        functools.partial(local_kernel, (gw, gt, entries, UNROLLED)),
        name="local_pairs",
        out_shape=stack(total),
        in_specs=[HBM] * 5,
        out_specs=HBM,
        scratch_shapes=[
            pltpu.SMEM((entries * gw, 128), i32),
            buffer((gw + 2) * gt),
            pltpu.VMEM(kernels.shape, bf16),
            buffer(bank * step + 1),
            buffer(bank * step + 1),
            buffer(total),
            pltpu.SemaphoreType.DMA((7,)),
        ],
        compiler_params=pltpu.CompilerParams(vmem_limit_bytes=44 * MIB),
        cost_estimate=cost(2 * (gw + 2) * gt * channels * tile * tile * bank, 30),
    )(local_index, tiles, near, far, kernels)

    count = len(received)
    rates, wall_out = pl.pallas_call(
        functools.partial(finish_kernel, (gw, gt, entries, peers, cap, walls, merged)),
        name="columns_and_walls",
        out_shape=(jax.ShapeDtypeStruct((gw, gt, channels, tile), bf16), stack(walls)),
        in_specs=[SMEM, SMEM] + [VMEM] * (3 + count) + [HBM],
        out_specs=(HBM, VMEM),
        scratch_shapes=[
            buffer(bank * 2 * depth + 1),
            buffer(wall_bank * peers * cap + 1),
            pltpu.VMEM((2, gw, channels, tile), bf16),
            pltpu.SemaphoreType.DMA((2,)),
            pltpu.SemaphoreType.DMA((2,)),
        ],
        input_output_aliases={5 + count: 0},
        compiler_params=pltpu.CompilerParams(vmem_limit_bytes=44 * MIB),
        cost_estimate=cost(2 * peers * cap * channels * tile * tile * wall_bank, 8),
    )(
        side_index,
        wall_index,
        own,
        *received,
        kernels,
        wall_kernels,
        rates.reshape(gw, gt, channels, tile),
    )
    return rates, wall_out.reshape(1, 1, walls, channels, tile)


def solution(mesh):
    in_specs = (
        P("weld", "trans", None, None),
        P("weld", "trans", None),
        P("weld", "trans", None),
        P(),
        P("weld", "trans", None, None),
        P("weld", "trans", None, None),
        P("weld", "trans", None, None),
        P(),
    )
    out_specs = (P("weld", "trans", None, None), P("weld", "trans", None, None, None))
    return jax.shard_map(
        on_device, mesh=mesh, in_specs=in_specs, out_specs=out_specs, check_vma=False
    )
```

```python
import functools

import jax
import jax.numpy as jnp
from jax import lax
from jax.experimental import pallas as pl
from jax.experimental.pallas import tpu as pltpu
from jax.sharding import PartitionSpec as P

SMEM = pl.BlockSpec(memory_space=pltpu.SMEM)
VMEM = pl.BlockSpec(memory_space=pltpu.VMEM)
HBM = pl.BlockSpec(memory_space=pl.ANY)
MIB = 1 << 20
UNROLLED = False
WALL_LANE = 64


def pick(cond, a, b):
    return lax.select(cond, jnp.int32(a), jnp.int32(b))


def index_kernel(dims, off_ref, kind_ref, slot_ref, wkind_ref, local_ref, side_ref):
    gw, gt, bank, wall_bank, peers, cap = dims
    t = lax.axis_index("trans")
    off, kind = off_ref[...], kind_ref[...]
    dr = (off * 11) >> 5
    row = lax.broadcasted_iota(jnp.int32, off.shape, 1)
    band = row + dr - jnp.where(row < gw // 2, 0, gw // 2)
    col = lax.broadcasted_iota(jnp.int32, off.shape, 2) + (off - 3 * dr) - 1
    left, right = col < 0, col >= gt
    side = left | right
    rows = gw // 2 + 2
    local_ref[:, :, :gt] = jnp.where(
        side, bank * rows * gt, kind * (rows * gt) + band * gt + col
    )
    even_t = lax.rem(t, 2) == 0
    depth = gw + 2
    base = jnp.where(left, pick(even_t, depth, 0), pick(even_t, 0, depth))
    edge = (left & (t == 0)) | (right & (t == peers - 1))
    side_ref[:, :, :gt] = jnp.where(
        side & ~edge, kind * (2 * depth) + base + row + dr, bank * 2 * depth
    )
    slot = slot_ref[...]
    sender = slot // cap
    wall = jnp.where(
        slot >= peers * cap,
        wall_bank * peers * cap,
        wkind_ref[...] * (peers * cap) + (sender ^ t) * cap + (slot - sender * cap),
    )
    for q in range(slot.shape[0] // gw):
        side_ref[q, :, WALL_LANE : WALL_LANE + slot.shape[1]] = wall[q * gw : (q + 1) * gw]


def load_tiles(x_ref, held_ref, sem):
    count = x_ref.shape[0]
    return pltpu.make_async_copy(x_ref, held_ref.at[:count], sem)


def blank(ref):
    ref[ref.shape[0] - 1] = jnp.zeros(ref.shape[1:], ref.dtype)


def listed(held_ref, list_ref, owner, out_ref):
    for c in range(list_ref.shape[1]):
        out_ref[c] = held_ref[list_ref[owner, c]]


def first_kernel(dims, early, list_ref, x_ref, near_ref, far_ref, *refs):
    gw, gt = dims
    outs, (held_ref, sem) = refs[: len(early)], refs[len(early) :]
    w, t = lax.axis_index("weld"), lax.axis_index("trans")
    even = lax.rem(w, 2) == 0

    def span(first, count):
        return pl.ds(first * gt, count * gt)

    loads = [
        pltpu.make_async_copy(x_ref.at[at], held_ref.at[at], sem.at[i])
        for i, at in enumerate((span(0, 1), span(gw - 1, 1), span(1, gw - 2)))
    ]
    for copy in loads:
        copy.start()
    blank(held_ref)
    loads[0].wait()
    loads[1].wait()
    rows = [
        pltpu.make_async_copy(held_ref.at[span(row, 1)], ref, sem.at[3 + i])
        for i, (ref, row) in enumerate(
            ((near_ref, pick(even, gw - 1, 0)), (far_ref, pick(even, 0, gw - 1)))
        )
    ]
    for copy in rows:
        copy.start()
    loads[2].wait()
    for k, ref in zip(early, outs):
        listed(held_ref, list_ref, t ^ k, ref)
    for copy in rows:
        copy.wait()


def second_kernel(dims, late, merged, list_ref, x_ref, near_ref, far_ref, *refs):
    gw, gt, cap = dims
    outs, (held_ref, sem, corner_sem) = refs[:-3], refs[-3:]
    w, t = lax.axis_index("weld"), lax.axis_index("trans")
    load = load_tiles(x_ref, held_ref, sem)
    load.start()
    blank(held_ref)
    corners, columns = [], []
    even_w, even_t = lax.rem(w, 2) == 0, lax.rem(t, 2) == 0
    for which in range(2):
        if merged:
            ref, base = outs[late.index((1, 3)[which])], cap
        else:
            ref, base = outs[len(late) + which], 0
        column = pick(even_t, gt - 1, 0) if which == 0 else pick(even_t, 0, gt - 1)
        for i, (corner, place) in enumerate(
            ((near_ref, pick(even_w, gw + 1, 0)), (far_ref, pick(even_w, 0, gw + 1)))
        ):
            copy = pltpu.make_async_copy(
                corner.at[column], ref.at[base + place], corner_sem.at[2 * which + i]
            )
            copy.start()
            corners.append(copy)
        columns.append((ref, base, column))
    load.wait()
    for ref, base, column in columns:
        for r in range(gw):
            ref[base + 1 + r] = held_ref[r * gt + column]
    for k, ref in zip(late, outs):
        listed(held_ref, list_ref, t ^ k, ref)
    for copy in corners:
        copy.wait()


def tree(terms):
    while len(terms) > 1:
        terms = [sum(terms[i : i + 2][1:], terms[i]) for i in range(0, len(terms), 2)]
    return terms[0]


def products(rows, bank_ref, j, targets):
    tiles = rows.shape[0] // 16
    both = jnp.concatenate([bank_ref[j], bank_ref[j + 1]], axis=1)
    wide = jnp.dot(rows, both, preferred_element_type=jnp.float32).astype(jnp.bfloat16)
    for h in range(2):
        part = wide[:, 128 * h : 128 * (h + 1)].reshape(tiles, 16, 128)
        for ref, step, at, low, count in targets:
            start = (j + h) * step + at
            ref[start : start + count] = part[low : low + count]


def local_kernel(dims, index_ref, x_ref, near_ref, far_ref, bank, out_ref, *scratch):
    gw, gt, entries, unrolled = dims
    index, top, low, total, index_sem, sem = scratch
    even = lax.rem(lax.axis_index("weld"), 2) == 0
    half, kernels = gw // 2, bank.shape[0]
    step = (half + 2) * gt
    fetch = pltpu.make_async_copy(index_ref, index, index_sem)
    fetch.start()
    blank(top)
    blank(low)
    before = jnp.where(even, far_ref[...], near_ref[...])
    after = jnp.where(even, near_ref[...], far_ref[...])

    def gather(table, r, c):
        terms = [table[index[n * gw + r, c]].astype(jnp.float32) for n in range(entries)]
        total[r * gt + c] = tree(terms).astype(total.dtype)

    upper = [(top, step, 0, 0, step), (low, step, 0, half * gt, 2 * gt)]
    lower = [(low, step, 2 * gt, 0, half * gt)]
    cut = (half + 1) * gt
    first = jnp.concatenate([before, x_ref[:cut]], axis=0).reshape(step * 16, 128)
    for j in range(0, kernels, 2):
        products(first, bank, j, upper)
    fetch.wait()
    second = jnp.concatenate([x_ref[cut:], after], axis=0).reshape(half * gt * 16, 128)
    cells = [(r, c) for r in range(half) for c in range(gt)]
    share = len(cells) * 2 // kernels
    for j in range(0, kernels, 2):
        products(second, bank, j, lower)
        if unrolled:
            for r, c in cells[j // 2 * share : (j // 2 + 1) * share]:
                gather(top, r, c)

    def store(first, count, i):
        span = pl.ds(first * gt, count * gt)
        copy = pltpu.make_async_copy(total.at[span], out_ref.at[span], sem.at[i])
        copy.start()
        return copy

    def body(r, _, table):
        for c in range(gt):
            gather(table, r, c)
        return 0

    if not unrolled:
        lax.fori_loop(0, half, functools.partial(body, table=top), 0)
    stores = [store(0, half, 0)]
    for i, first in enumerate(range(half, gw, half // 2)):
        if unrolled:
            for r in range(first, first + half // 2):
                body(r, 0, low)
        else:
            lax.fori_loop(first, first + half // 2, functools.partial(body, table=low), 0)
        stores.append(store(first, half // 2, 1 + i))
    for copy in stores:
        copy.wait()


def finish_kernel(dims, side_hbm, *refs):
    gw, gt, entries, peers, cap, walls, picks, merged = dims
    own_ref = refs[0]
    count = peers - 1 + (0 if merged else 2)
    got = refs[1 : 1 + count]
    bank_ref, wall_bank_ref, _, rates_ref, walls_ref = refs[1 + count : 6 + count]
    side_ref, table_ref, wall_table_ref, cols_ref, in_sem, out_sem = refs[6 + count :]
    edges = [(rates_ref.at[:, c], cols_ref.at[e]) for e, c in enumerate((0, gt - 1))]
    fetch = [pltpu.make_async_copy(a, b, in_sem.at[e]) for e, (a, b) in enumerate(edges)]
    store = [pltpu.make_async_copy(b, a, out_sem.at[e]) for e, (a, b) in enumerate(edges)]
    fetch.append(pltpu.make_async_copy(side_hbm, side_ref, in_sem.at[2]))
    for copy in fetch:
        copy.start()
    depth = gw + 2
    if merged:
        sides = [got[0][cap : cap + depth], got[2][cap : cap + depth]]
    else:
        sides = [got[-2][...], got[-1][...]]
    blank(table_ref)
    blank(wall_table_ref)
    ring = jnp.concatenate(sides, axis=0).reshape(2 * depth * 16, 128)
    for j in range(0, bank_ref.shape[0], 2):
        products(ring, bank_ref, j, [(table_ref, 2 * depth, 0, 0, 2 * depth)])
    slots = peers * cap
    received = jnp.concatenate([own_ref[...]] + [g[:cap] for g in got[: peers - 1]], axis=0)
    received = received.reshape(slots * 16, 128)
    for j in range(0, wall_bank_ref.shape[0], 2):
        products(received, wall_bank_ref, j, [(wall_table_ref, slots, 0, 0, slots)])
    for copy in fetch:
        copy.wait()
    for e, c in enumerate((0, gt - 1)):
        for r in range(gw):
            terms = [
                table_ref[side_ref[n * gw + r, c]].astype(jnp.float32) for n in range(entries)
            ]
            base = cols_ref[e, r].astype(jnp.float32)
            cols_ref[e, r] = (base + tree(terms)).astype(cols_ref.dtype)
        store[e].start()
    for j in range(walls):
        picked = [
            wall_table_ref[side_ref[j, WALL_LANE + m]].astype(jnp.float32) for m in range(picks)
        ]
        sums = tree(picked)
        walls_ref[j] = (sums / (1.0 + sums[0:1, :])).astype(walls_ref.dtype)
    for copy in store:
        copy.wait()


def pairing(count, shift):
    pairs = []
    for low in range(shift, count - 1, 2):
        pairs += [(low, low + 1), (low + 1, low)]
    return pairs


def on_device(
    features, pair_offsets, pair_kernel, kernels, send_list, wall_slots, wall_kernel, wall_kernels
):
    gw, gt, channels, tile = features.shape
    entries = pair_offsets.shape[2]
    bank, wall_bank = kernels.shape[0], wall_kernels.shape[0]
    peers, cap = send_list.shape[2:]
    walls, picks = wall_slots.shape[2:]
    weld = lax.axis_size("weld")
    merged = peers == 4
    depth = gw + 2
    i32, bf16 = jnp.int32, jnp.bfloat16
    total = gw * gt
    tiles = features.reshape(total, channels, tile)
    lists = send_list.reshape(peers, cap)

    def stack(n):
        return jax.ShapeDtypeStruct((n, channels, tile), bf16)

    def buffer(n):
        return pltpu.VMEM((n, channels, tile), bf16)

    def cost(flops, mib):
        return pl.CostEstimate(flops=flops, bytes_accessed=mib * MIB, transcendentals=0)

    early = (2,) if merged else tuple(range(2, peers))
    late = (1, 3, 0) if merged else (1, 0)
    near_out, far_out, *early_out = pl.pallas_call(
        functools.partial(first_kernel, (gw, gt), early),
        name="edge_rows",
        out_shape=(stack(gt), stack(gt)) + (stack(cap),) * len(early),
        in_specs=[SMEM, HBM],
        out_specs=(HBM, HBM) + (VMEM,) * len(early),
        scratch_shapes=[buffer(total + 1), pltpu.SemaphoreType.DMA((5,))],
        cost_estimate=cost(0, 2),
    )(lists, tiles)
    near = lax.ppermute(near_out, "weld", pairing(weld, 0))
    far = lax.ppermute(far_out, "weld", pairing(weld, 1))
    got = {}
    for k, message in zip(early, early_out):
        got[k] = lax.ppermute(message, "trans", [(i, i ^ k) for i in range(peers)])

    table_index = jax.ShapeDtypeStruct((entries, gw, 128), i32)
    local_index, side_index = pl.pallas_call(
        functools.partial(index_kernel, (gw, gt, bank, wall_bank, peers, cap)),
        name="pair_index",
        out_shape=(table_index, table_index),
        in_specs=[VMEM] * 4,
        out_specs=(VMEM, VMEM),
        cost_estimate=cost(1_000_000, 3),
    )(
        pair_offsets.transpose(2, 0, 1),
        pair_kernel.transpose(2, 0, 1),
        wall_slots.reshape(walls, picks),
        wall_kernel.reshape(walls, picks),
    )
    local_index = local_index.reshape(entries * gw, 128)
    side_index = side_index.reshape(entries * gw, 128)

    lengths = [cap + (depth if merged and k else 0) for k in late]
    if not merged:
        lengths += [depth, depth]
    late_out = pl.pallas_call(
        functools.partial(second_kernel, (gw, gt, cap), late, merged),
        name="edge_columns",
        out_shape=tuple(stack(n) for n in lengths),
        in_specs=[SMEM, HBM, HBM, HBM],
        out_specs=(VMEM,) * len(lengths),
        scratch_shapes=[
            buffer(total + 1),
            pltpu.SemaphoreType.DMA,
            pltpu.SemaphoreType.DMA((4,)),
        ],
        compiler_params=pltpu.CompilerParams(vmem_limit_bytes=8 * MIB),
        cost_estimate=cost(0, 2),
    )(lists, tiles, near, far)
    for k, message in zip(late, late_out):
        if k:
            got[k] = lax.ppermute(message, "trans", [(i, i ^ k) for i in range(peers)])
    own = late_out[late.index(0)]
    received = [got[k] for k in range(1, peers)]
    if not merged:
        received += [
            lax.ppermute(late_out[len(late) + s], "trans", pairing(peers, s)) for s in range(2)
        ]

    step = (gw // 2 + 2) * gt
    rates = pl.pallas_call(
        functools.partial(local_kernel, (gw, gt, entries, UNROLLED)),
        name="local_pairs",
        out_shape=stack(total),
        in_specs=[HBM] + [VMEM] * 4,
        out_specs=HBM,
        scratch_shapes=[
            pltpu.SMEM((entries * gw, 128), i32),
            buffer(bank * step + 1),
            buffer(bank * step + 1),
            buffer(total),
            pltpu.SemaphoreType.DMA,
            pltpu.SemaphoreType.DMA((3,)),
        ],
        compiler_params=pltpu.CompilerParams(vmem_limit_bytes=44 * MIB),
        cost_estimate=cost(2 * (gw + 2) * gt * channels * tile * tile * bank, 30),
    )(local_index, tiles, near, far, kernels)

    count = len(received)
    rates, wall_out = pl.pallas_call(
        functools.partial(finish_kernel, (gw, gt, entries, peers, cap, walls, picks, merged)),
        name="columns_and_walls",
        out_shape=(jax.ShapeDtypeStruct((gw, gt, channels, tile), bf16), stack(walls)),
        in_specs=[HBM] + [VMEM] * (3 + count) + [HBM],
        out_specs=(HBM, VMEM),
        scratch_shapes=[
            pltpu.SMEM((entries * gw, 128), i32),
            buffer(bank * 2 * depth + 1),
            buffer(wall_bank * peers * cap + 1),
            pltpu.VMEM((2, gw, channels, tile), bf16),
            pltpu.SemaphoreType.DMA((3,)),
            pltpu.SemaphoreType.DMA((2,)),
        ],
        input_output_aliases={4 + count: 0},
        compiler_params=pltpu.CompilerParams(vmem_limit_bytes=44 * MIB),
        cost_estimate=cost(2 * peers * cap * channels * tile * tile * wall_bank, 8),
    )(
        side_index,
        own,
        *received,
        kernels,
        wall_kernels,
        rates.reshape(gw, gt, channels, tile),
    )
    return rates, wall_out.reshape(1, 1, walls, channels, tile)


def solution(mesh):
    in_specs = (
        P("weld", "trans", None, None),
        P("weld", "trans", None),
        P("weld", "trans", None),
        P(),
        P("weld", "trans", None, None),
        P("weld", "trans", None, None),
        P("weld", "trans", None, None),
        P(),
    )
    out_specs = (P("weld", "trans", None, None), P("weld", "trans", None, None, None))
    return jax.shard_map(
        on_device, mesh=mesh, in_specs=in_specs, out_specs=out_specs, check_vma=False
    )
```

```python
import functools

import jax
import jax.numpy as jnp
from jax import lax
from jax.experimental import pallas as pl
from jax.experimental.pallas import tpu as pltpu
from jax.sharding import PartitionSpec as P

SMEM = pl.BlockSpec(memory_space=pltpu.SMEM)
VMEM = pl.BlockSpec(memory_space=pltpu.VMEM)
HBM = pl.BlockSpec(memory_space=pl.ANY)
MIB = 1 << 20
UNROLLED = True
WALL_LANE = 64


def pick(cond, a, b):
    return lax.select(cond, jnp.int32(a), jnp.int32(b))


def index_kernel(dims, off_ref, kind_ref, slot_ref, wkind_ref, local_ref, side_ref):
    gw, gt, bank, wall_bank, peers, cap = dims
    t = lax.axis_index("trans")
    off, kind = off_ref[...], kind_ref[...]
    dr = (off * 11) >> 5
    row = lax.broadcasted_iota(jnp.int32, off.shape, 1)
    band = row + dr - jnp.where(row < gw // 2, 0, gw // 2)
    col = lax.broadcasted_iota(jnp.int32, off.shape, 2) + (off - 3 * dr) - 1
    left, right = col < 0, col >= gt
    side = left | right
    rows = gw // 2 + 2
    local_ref[:, :, :gt] = jnp.where(
        side, bank * rows * gt, kind * (rows * gt) + band * gt + col
    )
    even_t = lax.rem(t, 2) == 0
    depth = gw + 2
    base = jnp.where(left, pick(even_t, depth, 0), pick(even_t, 0, depth))
    edge = (left & (t == 0)) | (right & (t == peers - 1))
    side_ref[:, :, :gt] = jnp.where(
        side & ~edge, kind * (2 * depth) + base + row + dr, bank * 2 * depth
    )
    slot = slot_ref[...]
    sender = slot // cap
    wall = jnp.where(
        slot >= peers * cap,
        wall_bank * peers * cap,
        wkind_ref[...] * (peers * cap) + (sender ^ t) * cap + (slot - sender * cap),
    )
    for q in range(slot.shape[0] // gw):
        side_ref[q, :, WALL_LANE : WALL_LANE + slot.shape[1]] = wall[q * gw : (q + 1) * gw]


def blank(ref):
    ref[ref.shape[0] - 1] = jnp.zeros(ref.shape[1:], ref.dtype)


def listed(held_ref, count, list_ref, owner, out_ref):
    empty = jnp.zeros(held_ref.shape[1:], held_ref.dtype)
    for c in range(list_ref.shape[1]):
        item = list_ref[owner, c]
        tile = held_ref[jnp.minimum(item, count - 1)]
        out_ref[c] = jnp.where(item < count, tile, empty)


def first_kernel(dims, early, list_ref, x_ref, near_ref, far_ref, *refs):
    gw, gt = dims
    outs, (picks_ref, held_ref, sem) = refs[: len(early)], refs[len(early) :]
    w, t = lax.axis_index("weld"), lax.axis_index("trans")
    even = lax.rem(w, 2) == 0

    def span(first, count):
        return pl.ds(first * gt, count * gt)

    loads = [
        pltpu.make_async_copy(x_ref.at[at], held_ref.at[at], sem.at[i])
        for i, at in enumerate((span(0, 1), span(gw - 1, 1), span(1, gw - 2)))
    ]
    loads.append(pltpu.make_async_copy(list_ref, picks_ref, sem.at[5]))
    for copy in loads:
        copy.start()
    loads[0].wait()
    loads[1].wait()
    near_ref[...] = held_ref[span(pick(even, gw - 1, 0), 1)]
    far_ref[...] = held_ref[span(pick(even, 0, gw - 1), 1)]
    loads[2].wait()
    loads[3].wait()
    for k, ref in zip(early, outs):
        listed(held_ref, gw * gt, picks_ref, t ^ k, ref)


def second_kernel(dims, late, merged, list_ref, held_ref, near_ref, far_ref, *outs):
    gw, gt, cap = dims
    w, t = lax.axis_index("weld"), lax.axis_index("trans")
    even_w, even_t = lax.rem(w, 2) == 0, lax.rem(t, 2) == 0
    for which in range(2):
        if merged:
            ref, base = outs[late.index((1, 3)[which])], cap
        else:
            ref, base = outs[len(late) + which], 0
        column = pick(even_t, gt - 1, 0) if which == 0 else pick(even_t, 0, gt - 1)
        ref[base + pick(even_w, gw + 1, 0)] = near_ref[column]
        ref[base + pick(even_w, 0, gw + 1)] = far_ref[column]
        for r in range(gw):
            ref[base + 1 + r] = held_ref[r * gt + column]
    for k, ref in zip(late, outs):
        listed(held_ref, gw * gt, list_ref, t ^ k, ref)


def tree(terms):
    while len(terms) > 1:
        terms = [sum(terms[i : i + 2][1:], terms[i]) for i in range(0, len(terms), 2)]
    return terms[0]


def products(rows, bank_ref, j, targets):
    tiles = rows.shape[0] // 16
    both = jnp.concatenate([bank_ref[j], bank_ref[j + 1]], axis=1)
    wide = jnp.dot(rows, both, preferred_element_type=jnp.float32).astype(jnp.bfloat16)
    for h in range(2):
        part = wide[:, 128 * h : 128 * (h + 1)].reshape(tiles, 16, 128)
        for ref, step, at, low, count in targets:
            start = (j + h) * step + at
            ref[start : start + count] = part[low : low + count]


def local_kernel(dims, index_ref, x_ref, near_ref, far_ref, bank, out_ref, *scratch):
    gw, gt, entries, unrolled = dims
    index, top, low, total, index_sem, sem = scratch
    even = lax.rem(lax.axis_index("weld"), 2) == 0
    half, kernels = gw // 2, bank.shape[0]
    step = (half + 2) * gt
    fetch = pltpu.make_async_copy(index_ref, index, index_sem)
    fetch.start()
    blank(top)
    blank(low)
    before = jnp.where(even, far_ref[...], near_ref[...])
    after = jnp.where(even, near_ref[...], far_ref[...])

    def gather(table, r, c):
        terms = [table[index[n * gw + r, c]].astype(jnp.float32) for n in range(entries)]
        total[r * gt + c] = tree(terms).astype(total.dtype)

    upper = [(top, step, 0, 0, step), (low, step, 0, half * gt, 2 * gt)]
    lower = [(low, step, 2 * gt, 0, half * gt)]
    cut = (half + 1) * gt
    first = jnp.concatenate([before, x_ref[:cut]], axis=0).reshape(step * 16, 128)
    for j in range(0, kernels, 2):
        products(first, bank, j, upper)
    fetch.wait()
    second = jnp.concatenate([x_ref[cut:], after], axis=0).reshape(half * gt * 16, 128)
    cells = [(r, c) for r in range(half) for c in range(gt)]
    share = len(cells) * 2 // kernels
    for j in range(0, kernels, 2):
        products(second, bank, j, lower)
        if unrolled:
            for r, c in cells[j // 2 * share : (j // 2 + 1) * share]:
                gather(top, r, c)

    def store(first, count, i):
        span = pl.ds(first * gt, count * gt)
        copy = pltpu.make_async_copy(total.at[span], out_ref.at[span], sem.at[i])
        copy.start()
        return copy

    def body(r, _, table):
        for c in range(gt):
            gather(table, r, c)
        return 0

    if not unrolled:
        lax.fori_loop(0, half, functools.partial(body, table=top), 0)
    stores = [store(0, half, 0)]
    for i, first in enumerate(range(half, gw, half // 2)):
        if unrolled:
            for r in range(first, first + half // 2):
                body(r, 0, low)
        else:
            lax.fori_loop(first, first + half // 2, functools.partial(body, table=low), 0)
        stores.append(store(first, half // 2, 1 + i))
    for copy in stores:
        copy.wait()


def finish_kernel(dims, side_hbm, *refs):
    gw, gt, entries, peers, cap, walls, picks, merged = dims
    own_ref = refs[0]
    count = peers - 1 + (0 if merged else 2)
    got = refs[1 : 1 + count]
    bank_ref, wall_bank_ref, _, rates_ref, walls_ref = refs[1 + count : 6 + count]
    side_ref, table_ref, wall_table_ref, cols_ref, in_sem, out_sem = refs[6 + count :]
    edges = [(rates_ref.at[:, c], cols_ref.at[e]) for e, c in enumerate((0, gt - 1))]
    fetch = [pltpu.make_async_copy(a, b, in_sem.at[e]) for e, (a, b) in enumerate(edges)]
    store = [pltpu.make_async_copy(b, a, out_sem.at[e]) for e, (a, b) in enumerate(edges)]
    fetch.append(pltpu.make_async_copy(side_hbm, side_ref, in_sem.at[2]))
    for copy in fetch:
        copy.start()
    depth = gw + 2
    if merged:
        sides = [got[0][cap : cap + depth], got[2][cap : cap + depth]]
    else:
        sides = [got[-2][...], got[-1][...]]
    blank(table_ref)
    blank(wall_table_ref)
    ring = jnp.concatenate(sides, axis=0).reshape(2 * depth * 16, 128)
    for j in range(0, bank_ref.shape[0], 2):
        products(ring, bank_ref, j, [(table_ref, 2 * depth, 0, 0, 2 * depth)])
    slots = peers * cap
    received = jnp.concatenate([own_ref[...]] + [g[:cap] for g in got[: peers - 1]], axis=0)
    received = received.reshape(slots * 16, 128)
    for j in range(0, wall_bank_ref.shape[0], 2):
        products(received, wall_bank_ref, j, [(wall_table_ref, slots, 0, 0, slots)])
    for copy in fetch:
        copy.wait()
    for e, c in enumerate((0, gt - 1)):
        for r in range(gw):
            terms = [
                table_ref[side_ref[n * gw + r, c]].astype(jnp.float32) for n in range(entries)
            ]
            base = cols_ref[e, r].astype(jnp.float32)
            cols_ref[e, r] = (base + tree(terms)).astype(cols_ref.dtype)
        store[e].start()
    for j in range(walls):
        picked = [
            wall_table_ref[side_ref[j, WALL_LANE + m]].astype(jnp.float32) for m in range(picks)
        ]
        sums = tree(picked)
        walls_ref[j] = (sums / (1.0 + sums[0:1, :])).astype(walls_ref.dtype)
    for copy in store:
        copy.wait()


def pairing(count, shift):
    pairs = []
    for low in range(shift, count - 1, 2):
        pairs += [(low, low + 1), (low + 1, low)]
    return pairs


def on_device(
    features, pair_offsets, pair_kernel, kernels, send_list, wall_slots, wall_kernel, wall_kernels
):
    gw, gt, channels, tile = features.shape
    entries = pair_offsets.shape[2]
    bank, wall_bank = kernels.shape[0], wall_kernels.shape[0]
    peers, cap = send_list.shape[2:]
    walls, picks = wall_slots.shape[2:]
    weld = lax.axis_size("weld")
    merged = peers == 4
    depth = gw + 2
    i32, bf16 = jnp.int32, jnp.bfloat16
    total = gw * gt
    tiles = features.reshape(total, channels, tile)
    lists = send_list.reshape(peers, cap)

    def stack(n):
        return jax.ShapeDtypeStruct((n, channels, tile), bf16)

    def buffer(n):
        return pltpu.VMEM((n, channels, tile), bf16)

    def cost(flops, mib):
        return pl.CostEstimate(flops=flops, bytes_accessed=mib * MIB, transcendentals=0)

    early = (2,) if merged else tuple(range(2, peers))
    late = (1, 3, 0) if merged else (1, 0)
    near_out, far_out, *early_out = pl.pallas_call(
        functools.partial(first_kernel, (gw, gt), early),
        name="edge_rows",
        out_shape=(stack(gt), stack(gt)) + (stack(cap),) * len(early),
        in_specs=[HBM, HBM],
        out_specs=(VMEM,) * (2 + len(early)),
        scratch_shapes=[
            pltpu.SMEM((peers, cap), i32),
            buffer(total),
            pltpu.SemaphoreType.DMA((6,)),
        ],
        compiler_params=pltpu.CompilerParams(vmem_limit_bytes=56 * MIB),
        cost_estimate=cost(0, 2),
    )(lists, tiles)
    near = lax.ppermute(near_out, "weld", pairing(weld, 0))
    far = lax.ppermute(far_out, "weld", pairing(weld, 1))
    got = {}
    for k, message in zip(early, early_out):
        got[k] = lax.ppermute(message, "trans", [(i, i ^ k) for i in range(peers)])

    table_index = jax.ShapeDtypeStruct((entries, gw, 128), i32)
    local_index, side_index = pl.pallas_call(
        functools.partial(index_kernel, (gw, gt, bank, wall_bank, peers, cap)),
        name="pair_index",
        out_shape=(table_index, table_index),
        in_specs=[VMEM] * 4,
        out_specs=(VMEM, VMEM),
        cost_estimate=cost(1_000_000, 3),
    )(
        pair_offsets.transpose(2, 0, 1),
        pair_kernel.transpose(2, 0, 1),
        wall_slots.reshape(walls, picks),
        wall_kernel.reshape(walls, picks),
    )
    local_index = local_index.reshape(entries * gw, 128)
    side_index = side_index.reshape(entries * gw, 128)

    lengths = [cap + (depth if merged and k else 0) for k in late]
    if not merged:
        lengths += [depth, depth]
    late_out = pl.pallas_call(
        functools.partial(second_kernel, (gw, gt, cap), late, merged),
        name="edge_columns",
        out_shape=tuple(stack(n) for n in lengths),
        in_specs=[SMEM, VMEM, VMEM, VMEM],
        out_specs=(VMEM,) * len(lengths),
        compiler_params=pltpu.CompilerParams(vmem_limit_bytes=8 * MIB),
        cost_estimate=cost(0, 2),
    )(lists, tiles, near, far)
    for k, message in zip(late, late_out):
        if k:
            got[k] = lax.ppermute(message, "trans", [(i, i ^ k) for i in range(peers)])
    own = late_out[late.index(0)]
    received = [got[k] for k in range(1, peers)]
    if not merged:
        received += [
            lax.ppermute(late_out[len(late) + s], "trans", pairing(peers, s)) for s in range(2)
        ]

    step = (gw // 2 + 2) * gt
    rates = pl.pallas_call(
        functools.partial(local_kernel, (gw, gt, entries, UNROLLED)),
        name="local_pairs",
        out_shape=stack(total),
        in_specs=[HBM] + [VMEM] * 4,
        out_specs=HBM,
        scratch_shapes=[
            pltpu.SMEM((entries * gw, 128), i32),
            buffer(bank * step + 1),
            buffer(bank * step + 1),
            buffer(total),
            pltpu.SemaphoreType.DMA,
            pltpu.SemaphoreType.DMA((3,)),
        ],
        compiler_params=pltpu.CompilerParams(vmem_limit_bytes=44 * MIB),
        cost_estimate=cost(2 * (gw + 2) * gt * channels * tile * tile * bank, 30),
    )(local_index, tiles, near, far, kernels)

    count = len(received)
    rates, wall_out = pl.pallas_call(
        functools.partial(finish_kernel, (gw, gt, entries, peers, cap, walls, picks, merged)),
        name="columns_and_walls",
        out_shape=(jax.ShapeDtypeStruct((gw, gt, channels, tile), bf16), stack(walls)),
        in_specs=[HBM] + [VMEM] * (3 + count) + [HBM],
        out_specs=(HBM, VMEM),
        scratch_shapes=[
            pltpu.SMEM((entries * gw, 128), i32),
            buffer(bank * 2 * depth + 1),
            buffer(wall_bank * peers * cap + 1),
            pltpu.VMEM((2, gw, channels, tile), bf16),
            pltpu.SemaphoreType.DMA((3,)),
            pltpu.SemaphoreType.DMA((2,)),
        ],
        input_output_aliases={4 + count: 0},
        compiler_params=pltpu.CompilerParams(vmem_limit_bytes=44 * MIB),
        cost_estimate=cost(2 * peers * cap * channels * tile * tile * wall_bank, 8),
    )(
        side_index,
        own,
        *received,
        kernels,
        wall_kernels,
        rates.reshape(gw, gt, channels, tile),
    )
    return rates, wall_out.reshape(1, 1, walls, channels, tile)


def solution(mesh):
    in_specs = (
        P("weld", "trans", None, None),
        P("weld", "trans", None),
        P("weld", "trans", None),
        P(),
        P("weld", "trans", None, None),
        P("weld", "trans", None, None),
        P("weld", "trans", None, None),
        P(),
    )
    out_specs = (P("weld", "trans", None, None), P("weld", "trans", None, None, None))
    return jax.shard_map(
        on_device, mesh=mesh, in_specs=in_specs, out_specs=out_specs, check_vma=False
    )
```

```python
import functools

import jax
import jax.numpy as jnp
from jax import lax
from jax.experimental import pallas as pl
from jax.experimental.pallas import tpu as pltpu
from jax.sharding import PartitionSpec as P

SMEM = pl.BlockSpec(memory_space=pltpu.SMEM)
VMEM = pl.BlockSpec(memory_space=pltpu.VMEM)
HBM = pl.BlockSpec(memory_space=pl.ANY)
MIB = 1 << 20
UNROLLED = True
LANES = 128
WALL_LANE = 32


def pick(cond, a, b):
    return lax.select(cond, jnp.int32(a), jnp.int32(b))


def index_kernel(dims, off_ref, kind_ref, slot_ref, wkind_ref, out_ref):
    gw, gt, bank, wall_bank, peers, cap = dims
    t = lax.axis_index("trans")
    off, kind = off_ref[...], kind_ref[...]
    dr = (off * 11) >> 5
    row = lax.broadcasted_iota(jnp.int32, off.shape, 1)
    band = row + dr - jnp.where(row < gw // 2, 0, gw // 2)
    col = lax.broadcasted_iota(jnp.int32, off.shape, 2) + (off - 3 * dr) - 1
    left, right = col < 0, col >= gt
    side = left | right
    rows = gw // 2 + 2
    local = jnp.where(side, bank * rows * gt, kind * (rows * gt) + band * gt + col)
    pack = LANES // gt
    for n in range(off.shape[0]):
        out_ref[n // pack, :, n % pack * gt : (n % pack + 1) * gt] = local[n]
    even_t = lax.rem(t, 2) == 0
    depth = gw + 2
    base = jnp.where(left, pick(even_t, depth, 0), pick(even_t, 0, depth))
    edge = (left & (t == 0)) | (right & (t == peers - 1))
    sides = jnp.where(side & ~edge, kind * (2 * depth) + base + row + dr, bank * 2 * depth)
    last = out_ref.shape[0] - 1
    for n in range(off.shape[0]):
        out_ref[last, :, 2 * n : 2 * n + 1] = sides[n, :, :1]
        out_ref[last, :, 2 * n + 1 : 2 * n + 2] = sides[n, :, gt - 1 :]
    slot = slot_ref[...]
    sender = slot // cap
    wall = jnp.where(
        slot >= peers * cap,
        wall_bank * peers * cap,
        wkind_ref[...] * (peers * cap) + (sender ^ t) * cap + (slot - sender * cap),
    )
    picks = slot.shape[1]
    for q in range(slot.shape[0] // gw):
        at = WALL_LANE + q * picks
        out_ref[last, :, at : at + picks] = wall[q * gw : (q + 1) * gw]


def blank(ref):
    ref[ref.shape[0] - 1] = jnp.zeros(ref.shape[1:], ref.dtype)


def listed(held_ref, count, list_ref, owner, out_ref):
    empty = jnp.zeros(held_ref.shape[1:], held_ref.dtype)
    for c in range(list_ref.shape[1]):
        item = list_ref[owner, c]
        tile = held_ref[jnp.minimum(item, count - 1)]
        out_ref[c] = jnp.where(item < count, tile, empty)


def first_kernel(dims, early, list_ref, x_ref, near_ref, far_ref, *refs):
    gw, gt = dims
    outs, (picks_ref, held_ref, sem) = refs[: len(early)], refs[len(early) :]
    w, t = lax.axis_index("weld"), lax.axis_index("trans")
    even = lax.rem(w, 2) == 0

    def span(first, count):
        return pl.ds(first * gt, count * gt)

    loads = [
        pltpu.make_async_copy(x_ref.at[at], held_ref.at[at], sem.at[i])
        for i, at in enumerate((span(0, 1), span(gw - 1, 1), span(1, gw - 2)))
    ]
    loads.append(pltpu.make_async_copy(list_ref, picks_ref, sem.at[5]))
    for copy in loads:
        copy.start()
    loads[0].wait()
    loads[1].wait()
    near_ref[...] = held_ref[span(pick(even, gw - 1, 0), 1)]
    far_ref[...] = held_ref[span(pick(even, 0, gw - 1), 1)]
    loads[2].wait()
    loads[3].wait()
    for k, ref in zip(early, outs):
        listed(held_ref, gw * gt, picks_ref, t ^ k, ref)


def second_kernel(dims, late, merged, list_ref, held_ref, near_ref, far_ref, *outs):
    gw, gt, cap = dims
    w, t = lax.axis_index("weld"), lax.axis_index("trans")
    even_w, even_t = lax.rem(w, 2) == 0, lax.rem(t, 2) == 0
    for which in range(2):
        if merged:
            ref, base = outs[late.index((1, 3)[which])], cap
        else:
            ref, base = outs[len(late) + which], 0
        column = pick(even_t, gt - 1, 0) if which == 0 else pick(even_t, 0, gt - 1)
        ref[base + pick(even_w, gw + 1, 0)] = near_ref[column]
        ref[base + pick(even_w, 0, gw + 1)] = far_ref[column]
        for r in range(gw):
            ref[base + 1 + r] = held_ref[r * gt + column]
    for k, ref in zip(late, outs):
        listed(held_ref, gw * gt, list_ref, t ^ k, ref)


def tree(terms):
    while len(terms) > 1:
        terms = [sum(terms[i : i + 2][1:], terms[i]) for i in range(0, len(terms), 2)]
    return terms[0]


def products(rows, bank_ref, j, targets):
    tiles = rows.shape[0] // 16
    both = jnp.concatenate([bank_ref[j], bank_ref[j + 1]], axis=1)
    wide = jnp.dot(rows, both, preferred_element_type=jnp.float32).astype(jnp.bfloat16)
    for h in range(2):
        part = wide[:, 128 * h : 128 * (h + 1)].reshape(tiles, 16, 128)
        for ref, step, at, low, count in targets:
            start = (j + h) * step + at
            ref[start : start + count] = part[low : low + count]


def local_kernel(dims, index_ref, x_ref, near_ref, far_ref, bank, out_ref, *scratch):
    gw, gt, entries, unrolled = dims
    index, top, low, sem = scratch
    pack = LANES // gt
    even = lax.rem(lax.axis_index("weld"), 2) == 0
    half, kernels = gw // 2, bank.shape[0]
    step = (half + 2) * gt
    fetch = pltpu.make_async_copy(index_ref.at[: entries // pack], index, sem)
    fetch.start()
    blank(top)
    blank(low)
    before = jnp.where(even, far_ref[...], near_ref[...])
    after = jnp.where(even, near_ref[...], far_ref[...])

    def gather(table, r, c):
        terms = [
            table[index[n // pack, r, n % pack * gt + c]].astype(jnp.float32)
            for n in range(entries)
        ]
        out_ref[r * gt + c] = tree(terms).astype(out_ref.dtype)

    upper = [(top, step, 0, 0, step), (low, step, 0, half * gt, 2 * gt)]
    lower = [(low, step, 2 * gt, 0, half * gt)]
    cut = (half + 1) * gt
    first = jnp.concatenate([before, x_ref[:cut]], axis=0).reshape(step * 16, 128)
    for j in range(0, kernels, 2):
        products(first, bank, j, upper)
    fetch.wait()
    second = jnp.concatenate([x_ref[cut:], after], axis=0).reshape(half * gt * 16, 128)
    cells = [(r, c) for r in range(half) for c in range(gt)]
    share = len(cells) * 2 // kernels
    for j in range(0, kernels, 2):
        products(second, bank, j, lower)
        if unrolled:
            for r, c in cells[j // 2 * share : (j // 2 + 1) * share]:
                gather(top, r, c)

    def body(r, _, table):
        for c in range(gt):
            gather(table, r, c)
        return 0

    if unrolled:
        for r in range(half, gw):
            body(r, 0, low)
    else:
        lax.fori_loop(0, half, functools.partial(body, table=top), 0)
        lax.fori_loop(half, gw, functools.partial(body, table=low), 0)


def finish_kernel(dims, index_ref, *refs):
    gw, gt, entries, peers, cap, walls, picks, merged = dims
    own_ref = refs[0]
    count = peers - 1 + (0 if merged else 2)
    got = refs[1 : 1 + count]
    bank_ref, wall_bank_ref, local_ref, rates_ref, walls_ref = refs[1 + count : 6 + count]
    index, table_ref, wall_table_ref, cols_ref, done_ref, sem = refs[6 + count :]
    fetch = pltpu.make_async_copy(index_ref.at[index_ref.shape[0] - 1], index, sem.at[0])
    inner = pltpu.make_async_copy(
        local_ref.at[:, 1 : gt - 1], rates_ref.at[:, 1 : gt - 1], sem.at[1]
    )
    edges = [
        pltpu.make_async_copy(cols_ref.at[e], rates_ref.at[:, c], sem.at[2 + e])
        for e, c in enumerate((0, gt - 1))
    ]
    part = walls // 2
    ready = [
        pltpu.make_async_copy(
            done_ref.at[pl.ds(h * part, part)], walls_ref.at[pl.ds(h * part, part)], sem.at[4 + h]
        )
        for h in range(2)
    ]
    fetch.start()
    inner.start()
    depth = gw + 2
    if merged:
        sides = [got[0][cap : cap + depth], got[2][cap : cap + depth]]
    else:
        sides = [got[-2][...], got[-1][...]]
    blank(table_ref)
    blank(wall_table_ref)
    ring = jnp.concatenate(sides, axis=0).reshape(2 * depth * 16, 128)
    for j in range(0, bank_ref.shape[0], 2):
        products(ring, bank_ref, j, [(table_ref, 2 * depth, 0, 0, 2 * depth)])
    slots = peers * cap
    received = jnp.concatenate([own_ref[...]] + [g[:cap] for g in got[: peers - 1]], axis=0)
    received = received.reshape(slots * 16, 128)
    for j in range(0, wall_bank_ref.shape[0], 2):
        products(received, wall_bank_ref, j, [(wall_table_ref, slots, 0, 0, slots)])
    fetch.wait()
    for e, c in enumerate((0, gt - 1)):
        for r in range(gw):
            terms = [table_ref[index[r, 2 * n + e]].astype(jnp.float32) for n in range(entries)]
            base = local_ref[r, c].astype(jnp.float32)
            cols_ref[e, r] = (base + tree(terms)).astype(cols_ref.dtype)
        edges[e].start()
    for j in range(walls):
        lane = WALL_LANE + j // gw * picks
        picked = [
            wall_table_ref[index[j % gw, lane + m]].astype(jnp.float32) for m in range(picks)
        ]
        sums = tree(picked)
        done_ref[j] = (sums / (1.0 + sums[0:1, :])).astype(done_ref.dtype)
        if (j + 1) % part == 0:
            ready[j // part].start()
    for copy in (inner, *edges, *ready):
        copy.wait()


def pairing(count, shift):
    pairs = []
    for low in range(shift, count - 1, 2):
        pairs += [(low, low + 1), (low + 1, low)]
    return pairs


def on_device(
    features, pair_offsets, pair_kernel, kernels, send_list, wall_slots, wall_kernel, wall_kernels
):
    gw, gt, channels, tile = features.shape
    entries = pair_offsets.shape[2]
    bank, wall_bank = kernels.shape[0], wall_kernels.shape[0]
    peers, cap = send_list.shape[2:]
    walls, picks = wall_slots.shape[2:]
    weld = lax.axis_size("weld")
    merged = peers == 4
    depth = gw + 2
    i32, bf16 = jnp.int32, jnp.bfloat16
    total = gw * gt
    tiles = features.reshape(total, channels, tile)
    lists = send_list.reshape(peers, cap)

    def stack(n):
        return jax.ShapeDtypeStruct((n, channels, tile), bf16)

    def buffer(n):
        return pltpu.VMEM((n, channels, tile), bf16)

    def cost(flops, mib):
        return pl.CostEstimate(flops=flops, bytes_accessed=mib * MIB, transcendentals=0)

    early = (2,) if merged else tuple(range(2, peers))
    late = (1, 3, 0) if merged else (1, 0)
    near_out, far_out, *early_out = pl.pallas_call(
        functools.partial(first_kernel, (gw, gt), early),
        name="edge_rows",
        out_shape=(stack(gt), stack(gt)) + (stack(cap),) * len(early),
        in_specs=[HBM, HBM],
        out_specs=(VMEM,) * (2 + len(early)),
        scratch_shapes=[
            pltpu.SMEM((peers, cap), i32),
            buffer(total),
            pltpu.SemaphoreType.DMA((6,)),
        ],
        compiler_params=pltpu.CompilerParams(vmem_limit_bytes=56 * MIB),
        cost_estimate=cost(0, 2),
    )(lists, tiles)
    near = lax.ppermute(near_out, "weld", pairing(weld, 0))
    far = lax.ppermute(far_out, "weld", pairing(weld, 1))
    got = {}
    for k, message in zip(early, early_out):
        got[k] = lax.ppermute(message, "trans", [(i, i ^ k) for i in range(peers)])

    planes = entries * gt // LANES + 1
    index = pl.pallas_call(
        functools.partial(index_kernel, (gw, gt, bank, wall_bank, peers, cap)),
        name="pair_index",
        out_shape=jax.ShapeDtypeStruct((planes, gw, LANES), i32),
        in_specs=[VMEM] * 4,
        out_specs=VMEM,
        cost_estimate=cost(1_000_000, 3),
    )(
        pair_offsets.transpose(2, 0, 1),
        pair_kernel.transpose(2, 0, 1),
        wall_slots.reshape(walls, picks),
        wall_kernel.reshape(walls, picks),
    )

    lengths = [cap + (depth if merged and k else 0) for k in late]
    if not merged:
        lengths += [depth, depth]
    late_out = pl.pallas_call(
        functools.partial(second_kernel, (gw, gt, cap), late, merged),
        name="edge_columns",
        out_shape=tuple(stack(n) for n in lengths),
        in_specs=[SMEM, VMEM, VMEM, VMEM],
        out_specs=(VMEM,) * len(lengths),
        compiler_params=pltpu.CompilerParams(vmem_limit_bytes=8 * MIB),
        cost_estimate=cost(0, 2),
    )(lists, tiles, near, far)
    for k, message in zip(late, late_out):
        if k:
            got[k] = lax.ppermute(message, "trans", [(i, i ^ k) for i in range(peers)])
    own = late_out[late.index(0)]
    received = [got[k] for k in range(1, peers)]
    if not merged:
        received += [
            lax.ppermute(late_out[len(late) + s], "trans", pairing(peers, s)) for s in range(2)
        ]

    step = (gw // 2 + 2) * gt
    rates = pl.pallas_call(
        functools.partial(local_kernel, (gw, gt, entries, UNROLLED)),
        name="local_pairs",
        out_shape=stack(total),
        in_specs=[HBM] + [VMEM] * 4,
        out_specs=VMEM,
        scratch_shapes=[
            pltpu.SMEM((planes - 1, gw, LANES), i32),
            buffer(bank * step + 1),
            buffer(bank * step + 1),
            pltpu.SemaphoreType.DMA,
        ],
        compiler_params=pltpu.CompilerParams(vmem_limit_bytes=44 * MIB),
        cost_estimate=cost(2 * (gw + 2) * gt * channels * tile * tile * bank, 30),
    )(index, tiles, near, far, kernels)

    count = len(received)
    rates, wall_out = pl.pallas_call(
        functools.partial(finish_kernel, (gw, gt, entries, peers, cap, walls, picks, merged)),
        name="columns_and_walls",
        out_shape=(jax.ShapeDtypeStruct((gw, gt, channels, tile), bf16), stack(walls)),
        in_specs=[HBM] + [VMEM] * (4 + count),
        out_specs=(HBM, HBM),
        scratch_shapes=[
            pltpu.SMEM((gw, LANES), i32),
            buffer(bank * 2 * depth + 1),
            buffer(wall_bank * peers * cap + 1),
            pltpu.VMEM((2, gw, channels, tile), bf16),
            buffer(walls),
            pltpu.SemaphoreType.DMA((6,)),
        ],
        compiler_params=pltpu.CompilerParams(vmem_limit_bytes=44 * MIB),
        cost_estimate=cost(2 * peers * cap * channels * tile * tile * wall_bank, 8),
    )(
        index,
        own,
        *received,
        kernels,
        wall_kernels,
        rates.reshape(gw, gt, channels, tile),
    )
    return rates, wall_out.reshape(1, 1, walls, channels, tile)


def solution(mesh):
    in_specs = (
        P("weld", "trans", None, None),
        P("weld", "trans", None),
        P("weld", "trans", None),
        P(),
        P("weld", "trans", None, None),
        P("weld", "trans", None, None),
        P("weld", "trans", None, None),
        P(),
    )
    out_specs = (P("weld", "trans", None, None), P("weld", "trans", None, None, None))
    return jax.shard_map(
        on_device, mesh=mesh, in_specs=in_specs, out_specs=out_specs, check_vma=False
    )
```

```python
import functools

import jax
import jax.numpy as jnp
from jax import lax
from jax.experimental import pallas as pl
from jax.experimental.pallas import tpu as pltpu
from jax.sharding import PartitionSpec as P

SMEM = pl.BlockSpec(memory_space=pltpu.SMEM)
VMEM = pl.BlockSpec(memory_space=pltpu.VMEM)
HBM = pl.BlockSpec(memory_space=pl.ANY)
MIB = 1 << 20
GROUPS = 2
LANES = 128
WALL_LANE = 32


def pick(cond, a, b):
    return lax.select(cond, jnp.int32(a), jnp.int32(b))


def index_kernel(dims, off_ref, kind_ref, slot_ref, wkind_ref, out_ref):
    gw, gt, bank, wall_bank, peers, cap = dims
    t = lax.axis_index("trans")
    off, kind = off_ref[...], kind_ref[...]
    dr = (off * 11) >> 5
    row = lax.broadcasted_iota(jnp.int32, off.shape, 1)
    per = gw // GROUPS
    band = lax.rem(row, per) + dr
    col = lax.broadcasted_iota(jnp.int32, off.shape, 2) + (off - 3 * dr) - 1
    left, right = col < 0, col >= gt
    side = left | right
    rows = per + 2
    local = jnp.where(side, bank * rows * gt, kind * (rows * gt) + band * gt + col)
    pack = LANES // gt
    for n in range(off.shape[0]):
        out_ref[n // pack, :, n % pack * gt : (n % pack + 1) * gt] = local[n]
    even_t = lax.rem(t, 2) == 0
    depth = gw + 2
    base = jnp.where(left, pick(even_t, depth, 0), pick(even_t, 0, depth))
    edge = (left & (t == 0)) | (right & (t == peers - 1))
    sides = jnp.where(side & ~edge, kind * (2 * depth) + base + row + dr, bank * 2 * depth)
    last = out_ref.shape[0] - 1
    for n in range(off.shape[0]):
        out_ref[last, :, 2 * n : 2 * n + 1] = sides[n, :, :1]
        out_ref[last, :, 2 * n + 1 : 2 * n + 2] = sides[n, :, gt - 1 :]
    slot = slot_ref[...]
    sender = slot // cap
    wall = jnp.where(
        slot >= peers * cap,
        wall_bank * peers * cap,
        wkind_ref[...] * (peers * cap) + (sender ^ t) * cap + (slot - sender * cap),
    )
    picks = slot.shape[1]
    for q in range(slot.shape[0] // gw):
        at = WALL_LANE + q * picks
        out_ref[last, :, at : at + picks] = wall[q * gw : (q + 1) * gw]


def blank(ref):
    ref[ref.shape[0] - 1] = jnp.zeros(ref.shape[1:], ref.dtype)


def listed(held_ref, count, list_ref, owner, out_ref):
    empty = jnp.zeros(held_ref.shape[1:], held_ref.dtype)
    for c in range(list_ref.shape[1]):
        item = list_ref[owner, c]
        tile = held_ref[jnp.minimum(item, count - 1)]
        out_ref[c] = jnp.where(item < count, tile, empty)


def first_kernel(dims, early, list_ref, x_ref, near_ref, far_ref, *refs):
    gw, gt = dims
    outs, (picks_ref, held_ref, sem) = refs[: len(early)], refs[len(early) :]
    w, t = lax.axis_index("weld"), lax.axis_index("trans")
    even = lax.rem(w, 2) == 0

    def span(first, count):
        return pl.ds(first * gt, count * gt)

    loads = [
        pltpu.make_async_copy(x_ref.at[at], held_ref.at[at], sem.at[i])
        for i, at in enumerate((span(0, 1), span(gw - 1, 1), span(1, gw - 2)))
    ]
    loads.append(pltpu.make_async_copy(list_ref, picks_ref, sem.at[5]))
    for copy in loads:
        copy.start()
    loads[0].wait()
    loads[1].wait()
    near_ref[...] = held_ref[span(pick(even, gw - 1, 0), 1)]
    far_ref[...] = held_ref[span(pick(even, 0, gw - 1), 1)]
    loads[2].wait()
    loads[3].wait()
    for k, ref in zip(early, outs):
        listed(held_ref, gw * gt, picks_ref, t ^ k, ref)


def second_kernel(dims, late, merged, list_ref, held_ref, near_ref, far_ref, *outs):
    gw, gt, cap = dims
    w, t = lax.axis_index("weld"), lax.axis_index("trans")
    even_w, even_t = lax.rem(w, 2) == 0, lax.rem(t, 2) == 0
    for which in range(2):
        if merged:
            ref, base = outs[late.index((1, 3)[which])], cap
        else:
            ref, base = outs[len(late) + which], 0
        column = pick(even_t, gt - 1, 0) if which == 0 else pick(even_t, 0, gt - 1)
        ref[base + pick(even_w, gw + 1, 0)] = near_ref[column]
        ref[base + pick(even_w, 0, gw + 1)] = far_ref[column]
        for r in range(gw):
            ref[base + 1 + r] = held_ref[r * gt + column]
    for k, ref in zip(late, outs):
        listed(held_ref, gw * gt, list_ref, t ^ k, ref)


def tree(terms):
    while len(terms) > 1:
        terms = [sum(terms[i : i + 2][1:], terms[i]) for i in range(0, len(terms), 2)]
    return terms[0]


def products(rows, bank_ref, j, targets):
    tiles = rows.shape[0] // 16
    both = jnp.concatenate([bank_ref[j], bank_ref[j + 1]], axis=1)
    wide = jnp.dot(rows, both, preferred_element_type=jnp.float32).astype(jnp.bfloat16)
    for h in range(2):
        part = wide[:, 128 * h : 128 * (h + 1)].reshape(tiles, 16, 128)
        for ref, step, at, low, count in targets:
            start = (j + h) * step + at
            ref[start : start + count] = part[low : low + count]


def local_kernel(dims, index_ref, x_ref, near_ref, far_ref, bank, out_ref, index, *scratch):
    gw, gt, entries = dims
    tables, sem = scratch[:-1], scratch[-1]
    pack = LANES // gt
    even = lax.rem(lax.axis_index("weld"), 2) == 0
    per, kernels = gw // GROUPS, bank.shape[0]
    step = (per + 2) * gt
    fetch = pltpu.make_async_copy(index_ref.at[: entries // pack], index, sem)
    fetch.start()
    for table in tables:
        blank(table)
    before = jnp.where(even, far_ref[...], near_ref[...])
    after = jnp.where(even, near_ref[...], far_ref[...])

    def gather(table, r, c):
        terms = [
            table[index[n // pack, r, n % pack * gt + c]].astype(jnp.float32)
            for n in range(entries)
        ]
        out_ref[r * gt + c] = tree(terms).astype(out_ref.dtype)

    share = per * gt * 2 // kernels
    for g, table in enumerate(tables):
        low, high = (0 if g == 0 else g * per + 2), g * per + per + 2
        parts = [before] if low == 0 else []
        parts.append(x_ref[max(low - 1, 0) * gt : min(high - 1, gw) * gt])
        if high == gw + 2:
            parts.append(after)
        rows = jnp.concatenate(parts, axis=0) if len(parts) > 1 else parts[0]
        fresh = (high - low) * gt
        targets = [(table, step, step - fresh, 0, fresh)]
        if g + 1 < GROUPS:
            targets.append((tables[g + 1], step, 0, fresh - 2 * gt, 2 * gt))
        cells = [((g - 1) * per + i // gt, i % gt) for i in range(per * gt)] if g else []
        for j in range(0, kernels, 2):
            products(rows.reshape(fresh * 16, 128), bank, j, targets)
            for r, c in cells[j // 2 * share : (j // 2 + 1) * share]:
                gather(tables[g - 1], r, c)
        if g == 0:
            fetch.wait()
    for r in range(gw - per, gw):
        for c in range(gt):
            gather(tables[-1], r, c)


def finish_kernel(dims, index_ref, *refs):
    gw, gt, entries, peers, cap, walls, picks, merged = dims
    own_ref = refs[0]
    count = peers - 1 + (0 if merged else 2)
    got = refs[1 : 1 + count]
    got = got[: peers - 1][::-1] + got[peers - 1 :]
    bank_ref, wall_bank_ref, local_ref, rates_ref, walls_ref = refs[1 + count : 6 + count]
    index, table_ref, wall_table_ref, cols_ref, done_ref, sem = refs[6 + count :]
    fetch = pltpu.make_async_copy(index_ref.at[index_ref.shape[0] - 1], index, sem.at[0])
    inner = pltpu.make_async_copy(
        local_ref.at[:, 1 : gt - 1], rates_ref.at[:, 1 : gt - 1], sem.at[1]
    )
    edges = [
        pltpu.make_async_copy(cols_ref.at[e], rates_ref.at[:, c], sem.at[2 + e])
        for e, c in enumerate((0, gt - 1))
    ]
    part = walls // 2
    ready = [
        pltpu.make_async_copy(
            done_ref.at[pl.ds(h * part, part)], walls_ref.at[pl.ds(h * part, part)], sem.at[4 + h]
        )
        for h in range(2)
    ]
    fetch.start()
    inner.start()
    depth = gw + 2
    if merged:
        sides = [got[0][cap : cap + depth], got[2][cap : cap + depth]]
    else:
        sides = [got[-2][...], got[-1][...]]
    blank(table_ref)
    blank(wall_table_ref)
    ring = jnp.concatenate(sides, axis=0).reshape(2 * depth * 16, 128)
    for j in range(0, bank_ref.shape[0], 2):
        products(ring, bank_ref, j, [(table_ref, 2 * depth, 0, 0, 2 * depth)])
    slots = peers * cap
    received = jnp.concatenate([own_ref[...]] + [g[:cap] for g in got[: peers - 1]], axis=0)
    received = received.reshape(slots * 16, 128)
    for j in range(0, wall_bank_ref.shape[0], 2):
        products(received, wall_bank_ref, j, [(wall_table_ref, slots, 0, 0, slots)])
    fetch.wait()
    for e, c in enumerate((0, gt - 1)):
        for r in range(gw):
            terms = [table_ref[index[r, 2 * n + e]].astype(jnp.float32) for n in range(entries)]
            base = local_ref[r, c].astype(jnp.float32)
            cols_ref[e, r] = (base + tree(terms)).astype(cols_ref.dtype)
        edges[e].start()
    for j in range(walls):
        lane = WALL_LANE + j // gw * picks
        picked = [
            wall_table_ref[index[j % gw, lane + m]].astype(jnp.float32) for m in range(picks)
        ]
        sums = tree(picked)
        done_ref[j] = (sums / (1.0 + sums[0:1, :])).astype(done_ref.dtype)
        if (j + 1) % part == 0:
            ready[j // part].start()
    for copy in (inner, *edges, *ready):
        copy.wait()


def pairing(count, shift):
    pairs = []
    for low in range(shift, count - 1, 2):
        pairs += [(low, low + 1), (low + 1, low)]
    return pairs


def on_device(
    features, pair_offsets, pair_kernel, kernels, send_list, wall_slots, wall_kernel, wall_kernels
):
    gw, gt, channels, tile = features.shape
    entries = pair_offsets.shape[2]
    bank, wall_bank = kernels.shape[0], wall_kernels.shape[0]
    peers, cap = send_list.shape[2:]
    walls, picks = wall_slots.shape[2:]
    weld = lax.axis_size("weld")
    merged = peers == 4
    depth = gw + 2
    i32, bf16 = jnp.int32, jnp.bfloat16
    total = gw * gt
    tiles = features.reshape(total, channels, tile)
    lists = send_list.reshape(peers, cap)

    def stack(n):
        return jax.ShapeDtypeStruct((n, channels, tile), bf16)

    def buffer(n):
        return pltpu.VMEM((n, channels, tile), bf16)

    def cost(flops, mib):
        return pl.CostEstimate(flops=flops, bytes_accessed=mib * MIB, transcendentals=0)

    early = (2,) if merged else tuple(range(2, peers))
    late = (1, 3, 0) if merged else (1, 0)
    near_out, far_out, *early_out = pl.pallas_call(
        functools.partial(first_kernel, (gw, gt), early),
        name="edge_rows",
        out_shape=(stack(gt), stack(gt)) + (stack(cap),) * len(early),
        in_specs=[HBM, HBM],
        out_specs=(VMEM,) * (2 + len(early)),
        scratch_shapes=[
            pltpu.SMEM((peers, cap), i32),
            buffer(total),
            pltpu.SemaphoreType.DMA((6,)),
        ],
        compiler_params=pltpu.CompilerParams(vmem_limit_bytes=56 * MIB),
        cost_estimate=cost(0, 2),
    )(lists, tiles)
    near = lax.ppermute(near_out, "weld", pairing(weld, 0))
    far = lax.ppermute(far_out, "weld", pairing(weld, 1))
    got = {}
    for k, message in zip(early, early_out):
        got[k] = lax.ppermute(message, "trans", [(i, i ^ k) for i in range(peers)])

    planes = entries * gt // LANES + 1
    index = pl.pallas_call(
        functools.partial(index_kernel, (gw, gt, bank, wall_bank, peers, cap)),
        name="pair_index",
        out_shape=jax.ShapeDtypeStruct((planes, gw, LANES), i32),
        in_specs=[VMEM] * 4,
        out_specs=VMEM,
        cost_estimate=cost(1_000_000, 3),
    )(
        pair_offsets.transpose(2, 0, 1),
        pair_kernel.transpose(2, 0, 1),
        wall_slots.reshape(walls, picks),
        wall_kernel.reshape(walls, picks),
    )

    lengths = [cap + (depth if merged and k else 0) for k in late]
    if not merged:
        lengths += [depth, depth]
    late_out = pl.pallas_call(
        functools.partial(second_kernel, (gw, gt, cap), late, merged),
        name="edge_columns",
        out_shape=tuple(stack(n) for n in lengths),
        in_specs=[SMEM, VMEM, VMEM, VMEM],
        out_specs=(VMEM,) * len(lengths),
        compiler_params=pltpu.CompilerParams(vmem_limit_bytes=8 * MIB),
        cost_estimate=cost(0, 2),
    )(lists, tiles, near, far)
    for k, message in zip(late, late_out):
        if k:
            got[k] = lax.ppermute(message, "trans", [(i, i ^ k) for i in range(peers)])
    own = late_out[late.index(0)]
    received = [got[k] for k in range(peers - 1, 0, -1)]
    if not merged:
        received += [
            lax.ppermute(late_out[len(late) + s], "trans", pairing(peers, s)) for s in range(2)
        ]

    step = (gw // GROUPS + 2) * gt
    rates = pl.pallas_call(
        functools.partial(local_kernel, (gw, gt, entries)),
        name="local_pairs",
        out_shape=stack(total),
        in_specs=[HBM] + [VMEM] * 4,
        out_specs=VMEM,
        scratch_shapes=[
            pltpu.SMEM((planes - 1, gw, LANES), i32),
            *[buffer(bank * step + 1)] * GROUPS,
            pltpu.SemaphoreType.DMA,
        ],
        compiler_params=pltpu.CompilerParams(vmem_limit_bytes=48 * MIB),
        cost_estimate=cost(2 * (gw + 2) * gt * channels * tile * tile * bank, 30),
    )(index, tiles, near, far, kernels)

    count = len(received)
    rates, wall_out = pl.pallas_call(
        functools.partial(finish_kernel, (gw, gt, entries, peers, cap, walls, picks, merged)),
        name="columns_and_walls",
        out_shape=(jax.ShapeDtypeStruct((gw, gt, channels, tile), bf16), stack(walls)),
        in_specs=[HBM] + [VMEM] * (4 + count),
        out_specs=(HBM, HBM),
        scratch_shapes=[
            pltpu.SMEM((gw, LANES), i32),
            buffer(bank * 2 * depth + 1),
            buffer(wall_bank * peers * cap + 1),
            pltpu.VMEM((2, gw, channels, tile), bf16),
            buffer(walls),
            pltpu.SemaphoreType.DMA((6,)),
        ],
        compiler_params=pltpu.CompilerParams(vmem_limit_bytes=44 * MIB),
        cost_estimate=cost(2 * peers * cap * channels * tile * tile * wall_bank, 8),
    )(
        index,
        own,
        *received,
        kernels,
        wall_kernels,
        rates.reshape(gw, gt, channels, tile),
    )
    return rates, wall_out.reshape(1, 1, walls, channels, tile)


def solution(mesh):
    in_specs = (
        P("weld", "trans", None, None),
        P("weld", "trans", None),
        P("weld", "trans", None),
        P(),
        P("weld", "trans", None, None),
        P("weld", "trans", None, None),
        P("weld", "trans", None, None),
        P(),
    )
    out_specs = (P("weld", "trans", None, None), P("weld", "trans", None, None, None))
    return jax.shard_map(
        on_device, mesh=mesh, in_specs=in_specs, out_specs=out_specs, check_vma=False
    )
```

```python
import functools

import jax
import jax.numpy as jnp
from jax import lax
from jax.experimental import pallas as pl
from jax.experimental.pallas import tpu as pltpu
from jax.sharding import PartitionSpec as P

SMEM = pl.BlockSpec(memory_space=pltpu.SMEM)
VMEM = pl.BlockSpec(memory_space=pltpu.VMEM)
HBM = pl.BlockSpec(memory_space=pl.ANY)
MIB = 1 << 20
GROUPS = 2
LANES = 128
WALL_LANE = 32


def pick(cond, a, b):
    return lax.select(cond, jnp.int32(a), jnp.int32(b))


def index_kernel(dims, off_ref, kind_ref, slot_ref, wkind_ref, out_ref):
    gw, gt, bank, wall_bank, peers, cap = dims
    t = lax.axis_index("trans")
    off, kind = off_ref[...], kind_ref[...]
    dr = (off * 11) >> 5
    row = lax.broadcasted_iota(jnp.int32, off.shape, 1)
    per = gw // GROUPS
    band = lax.rem(row, per) + dr
    col = lax.broadcasted_iota(jnp.int32, off.shape, 2) + (off - 3 * dr) - 1
    left, right = col < 0, col >= gt
    side = left | right
    rows = per + 2
    local = jnp.where(side, bank * rows * gt, kind * (rows * gt) + band * gt + col)
    pack = LANES // gt
    for n in range(off.shape[0]):
        out_ref[n // pack, :, n % pack * gt : (n % pack + 1) * gt] = local[n]
    even_t = lax.rem(t, 2) == 0
    depth = gw + 2
    base = jnp.where(left, pick(even_t, depth, 0), pick(even_t, 0, depth))
    edge = (left & (t == 0)) | (right & (t == peers - 1))
    sides = jnp.where(side & ~edge, kind * (2 * depth) + base + row + dr, bank * 2 * depth)
    last = out_ref.shape[0] - 1
    for n in range(off.shape[0]):
        out_ref[last, :, 2 * n : 2 * n + 1] = sides[n, :, :1]
        out_ref[last, :, 2 * n + 1 : 2 * n + 2] = sides[n, :, gt - 1 :]
    slot = slot_ref[...]
    sender = slot // cap
    wall = jnp.where(
        slot >= peers * cap,
        wall_bank * peers * cap,
        wkind_ref[...] * (peers * cap) + (sender ^ t) * cap + (slot - sender * cap),
    )
    picks = slot.shape[1]
    for q in range(slot.shape[0] // gw):
        at = WALL_LANE + q * picks
        out_ref[last, :, at : at + picks] = wall[q * gw : (q + 1) * gw]


def blank(ref):
    ref[ref.shape[0] - 1] = jnp.zeros(ref.shape[1:], ref.dtype)


def listed(held_ref, count, list_ref, owner, out_ref):
    empty = jnp.zeros(held_ref.shape[1:], held_ref.dtype)
    for c in range(list_ref.shape[1]):
        item = list_ref[owner, c]
        tile = held_ref[jnp.minimum(item, count - 1)]
        out_ref[c] = jnp.where(item < count, tile, empty)


def first_kernel(dims, early, list_ref, x_ref, near_ref, far_ref, *refs):
    gw, gt = dims
    outs, (picks_ref, held_ref, sem) = refs[: len(early)], refs[len(early) :]
    w, t = lax.axis_index("weld"), lax.axis_index("trans")
    even = lax.rem(w, 2) == 0

    def span(first, count):
        return pl.ds(first * gt, count * gt)

    half = gw // 2
    loads = [
        pltpu.make_async_copy(list_ref, picks_ref, sem.at[0]),
        pltpu.make_async_copy(x_ref.at[span(0, half)], held_ref.at[span(0, half)], sem.at[1]),
        pltpu.make_async_copy(
            x_ref.at[span(half, half)], held_ref.at[span(half, half)], sem.at[2]
        ),
    ]
    for copy in loads:
        copy.start()
    for copy in loads:
        copy.wait()
    near_ref[...] = held_ref[span(pick(even, gw - 1, 0), 1)]
    far_ref[...] = held_ref[span(pick(even, 0, gw - 1), 1)]
    for k, ref in zip(early, outs):
        listed(held_ref, gw * gt, picks_ref, t ^ k, ref)


def second_kernel(dims, late, merged, list_ref, held_ref, near_ref, far_ref, *outs):
    gw, gt, cap = dims
    w, t = lax.axis_index("weld"), lax.axis_index("trans")
    even_w, even_t = lax.rem(w, 2) == 0, lax.rem(t, 2) == 0
    for which in range(2):
        if merged:
            ref, base = outs[late.index((1, 3)[which])], cap
        else:
            ref, base = outs[len(late) + which], 0
        column = pick(even_t, gt - 1, 0) if which == 0 else pick(even_t, 0, gt - 1)
        ref[base + pick(even_w, gw + 1, 0)] = near_ref[column]
        ref[base + pick(even_w, 0, gw + 1)] = far_ref[column]
        for r in range(gw):
            ref[base + 1 + r] = held_ref[r * gt + column]
    for k, ref in zip(late, outs):
        listed(held_ref, gw * gt, list_ref, t ^ k, ref)


def tree(terms):
    while len(terms) > 1:
        terms = [sum(terms[i : i + 2][1:], terms[i]) for i in range(0, len(terms), 2)]
    return terms[0]


def products(rows, bank_ref, j, targets):
    tiles = rows.shape[0] // 16
    both = jnp.concatenate([bank_ref[j], bank_ref[j + 1]], axis=1)
    wide = jnp.dot(rows, both, preferred_element_type=jnp.float32).astype(jnp.bfloat16)
    for h in range(2):
        part = wide[:, 128 * h : 128 * (h + 1)].reshape(tiles, 16, 128)
        for ref, step, at, low, count in targets:
            start = (j + h) * step + at
            ref[start : start + count] = part[low : low + count]


def local_kernel(dims, index_ref, x_ref, near_ref, far_ref, bank, out_ref, index, *scratch):
    gw, gt, entries = dims
    tables, sem = scratch[:-1], scratch[-1]
    pack = LANES // gt
    even = lax.rem(lax.axis_index("weld"), 2) == 0
    per, kernels = gw // GROUPS, bank.shape[0]
    step = (per + 2) * gt
    fetch = pltpu.make_async_copy(index_ref.at[: entries // pack], index, sem)
    fetch.start()
    for table in tables:
        blank(table)
    before = jnp.where(even, far_ref[...], near_ref[...])
    after = jnp.where(even, near_ref[...], far_ref[...])

    def gather(table, r, c):
        terms = [
            table[index[n // pack, r, n % pack * gt + c]].astype(jnp.float32)
            for n in range(entries)
        ]
        out_ref[r * gt + c] = tree(terms).astype(out_ref.dtype)

    share = per * gt * 2 // kernels
    for g, table in enumerate(tables):
        low, high = (0 if g == 0 else g * per + 2), g * per + per + 2
        parts = [before] if low == 0 else []
        parts.append(x_ref[max(low - 1, 0) * gt : min(high - 1, gw) * gt])
        if high == gw + 2:
            parts.append(after)
        rows = jnp.concatenate(parts, axis=0) if len(parts) > 1 else parts[0]
        fresh = (high - low) * gt
        targets = [(table, step, step - fresh, 0, fresh)]
        if g + 1 < GROUPS:
            targets.append((tables[g + 1], step, 0, fresh - 2 * gt, 2 * gt))
        cells = [((g - 1) * per + i // gt, i % gt) for i in range(per * gt)] if g else []
        for j in range(0, kernels, 2):
            products(rows.reshape(fresh * 16, 128), bank, j, targets)
            for r, c in cells[j // 2 * share : (j // 2 + 1) * share]:
                gather(tables[g - 1], r, c)
        if g == 0:
            fetch.wait()
    for r in range(gw - per, gw):
        for c in range(gt):
            gather(tables[-1], r, c)


def finish_kernel(dims, index_ref, *refs):
    gw, gt, entries, peers, cap, walls, picks, merged = dims
    own_ref = refs[0]
    count = peers - 1 + (0 if merged else 2)
    got = refs[1 : 1 + count]
    got = got[: peers - 1][::-1] + got[peers - 1 :]
    bank_ref, wall_bank_ref, local_ref, rates_ref, walls_ref = refs[1 + count : 6 + count]
    index, table_ref, wall_table_ref, cols_ref, done_ref, sem = refs[6 + count :]
    fetch = pltpu.make_async_copy(index_ref.at[index_ref.shape[0] - 1], index, sem.at[0])
    inner = pltpu.make_async_copy(
        local_ref.at[:, 1 : gt - 1], rates_ref.at[:, 1 : gt - 1], sem.at[1]
    )
    edges = [
        pltpu.make_async_copy(cols_ref.at[e], rates_ref.at[:, c], sem.at[2 + e])
        for e, c in enumerate((0, gt - 1))
    ]
    part = walls // 2
    ready = [
        pltpu.make_async_copy(
            done_ref.at[pl.ds(h * part, part)], walls_ref.at[pl.ds(h * part, part)], sem.at[4 + h]
        )
        for h in range(2)
    ]
    fetch.start()
    inner.start()
    depth = gw + 2
    if merged:
        sides = [got[0][cap : cap + depth], got[2][cap : cap + depth]]
    else:
        sides = [got[-2][...], got[-1][...]]
    blank(table_ref)
    blank(wall_table_ref)
    ring = jnp.concatenate(sides, axis=0).reshape(2 * depth * 16, 128)
    for j in range(0, bank_ref.shape[0], 2):
        products(ring, bank_ref, j, [(table_ref, 2 * depth, 0, 0, 2 * depth)])
    slots = peers * cap
    received = jnp.concatenate([own_ref[...]] + [g[:cap] for g in got[: peers - 1]], axis=0)
    received = received.reshape(slots * 16, 128)
    for j in range(0, wall_bank_ref.shape[0], 2):
        products(received, wall_bank_ref, j, [(wall_table_ref, slots, 0, 0, slots)])
    fetch.wait()
    for e, c in enumerate((0, gt - 1)):
        for r in range(gw):
            terms = [table_ref[index[r, 2 * n + e]].astype(jnp.float32) for n in range(entries)]
            base = local_ref[r, c].astype(jnp.float32)
            cols_ref[e, r] = (base + tree(terms)).astype(cols_ref.dtype)
        edges[e].start()
    for j in range(walls):
        lane = WALL_LANE + j // gw * picks
        picked = [
            wall_table_ref[index[j % gw, lane + m]].astype(jnp.float32) for m in range(picks)
        ]
        sums = tree(picked)
        done_ref[j] = (sums / (1.0 + sums[0:1, :])).astype(done_ref.dtype)
        if (j + 1) % part == 0:
            ready[j // part].start()
    for copy in (inner, *edges, *ready):
        copy.wait()


def pairing(count, shift):
    pairs = []
    for low in range(shift, count - 1, 2):
        pairs += [(low, low + 1), (low + 1, low)]
    return pairs


def on_device(
    features, pair_offsets, pair_kernel, kernels, send_list, wall_slots, wall_kernel, wall_kernels
):
    gw, gt, channels, tile = features.shape
    entries = pair_offsets.shape[2]
    bank, wall_bank = kernels.shape[0], wall_kernels.shape[0]
    peers, cap = send_list.shape[2:]
    walls, picks = wall_slots.shape[2:]
    weld = lax.axis_size("weld")
    merged = peers == 4
    depth = gw + 2
    i32, bf16 = jnp.int32, jnp.bfloat16
    total = gw * gt
    tiles = features.reshape(total, channels, tile)
    lists = send_list.reshape(peers, cap)

    def stack(n):
        return jax.ShapeDtypeStruct((n, channels, tile), bf16)

    def buffer(n):
        return pltpu.VMEM((n, channels, tile), bf16)

    def cost(flops, mib):
        return pl.CostEstimate(flops=flops, bytes_accessed=mib * MIB, transcendentals=0)

    early = (2,) if merged else tuple(range(2, peers))
    late = (1, 3, 0) if merged else (1, 0)
    near_out, far_out, *early_out = pl.pallas_call(
        functools.partial(first_kernel, (gw, gt), early),
        name="edge_rows",
        out_shape=(stack(gt), stack(gt)) + (stack(cap),) * len(early),
        in_specs=[HBM, HBM],
        out_specs=(VMEM,) * (2 + len(early)),
        scratch_shapes=[
            pltpu.SMEM((peers, cap), i32),
            buffer(total),
            pltpu.SemaphoreType.DMA((3,)),
        ],
        compiler_params=pltpu.CompilerParams(vmem_limit_bytes=56 * MIB),
        cost_estimate=cost(0, 2),
    )(lists, tiles)
    near = lax.ppermute(near_out, "weld", pairing(weld, 0))
    far = lax.ppermute(far_out, "weld", pairing(weld, 1))
    got = {}
    for k, message in zip(early, early_out):
        got[k] = lax.ppermute(message, "trans", [(i, i ^ k) for i in range(peers)])

    planes = entries * gt // LANES + 1
    index = pl.pallas_call(
        functools.partial(index_kernel, (gw, gt, bank, wall_bank, peers, cap)),
        name="pair_index",
        out_shape=jax.ShapeDtypeStruct((planes, gw, LANES), i32),
        in_specs=[VMEM] * 4,
        out_specs=VMEM,
        cost_estimate=cost(1_000_000, 3),
    )(
        pair_offsets.transpose(2, 0, 1),
        pair_kernel.transpose(2, 0, 1),
        wall_slots.reshape(walls, picks),
        wall_kernel.reshape(walls, picks),
    )

    lengths = [cap + (depth if merged and k else 0) for k in late]
    if not merged:
        lengths += [depth, depth]
    late_out = pl.pallas_call(
        functools.partial(second_kernel, (gw, gt, cap), late, merged),
        name="edge_columns",
        out_shape=tuple(stack(n) for n in lengths),
        in_specs=[SMEM, VMEM, VMEM, VMEM],
        out_specs=(VMEM,) * len(lengths),
        compiler_params=pltpu.CompilerParams(vmem_limit_bytes=8 * MIB),
        cost_estimate=cost(0, 2),
    )(lists, tiles, near, far)
    for k, message in zip(late, late_out):
        if k:
            got[k] = lax.ppermute(message, "trans", [(i, i ^ k) for i in range(peers)])
    own = late_out[late.index(0)]
    received = [got[k] for k in range(peers - 1, 0, -1)]
    if not merged:
        received += [
            lax.ppermute(late_out[len(late) + s], "trans", pairing(peers, s)) for s in range(2)
        ]

    step = (gw // GROUPS + 2) * gt
    rates = pl.pallas_call(
        functools.partial(local_kernel, (gw, gt, entries)),
        name="local_pairs",
        out_shape=stack(total),
        in_specs=[HBM] + [VMEM] * 4,
        out_specs=VMEM,
        scratch_shapes=[
            pltpu.SMEM((planes - 1, gw, LANES), i32),
            *[buffer(bank * step + 1)] * GROUPS,
            pltpu.SemaphoreType.DMA,
        ],
        compiler_params=pltpu.CompilerParams(vmem_limit_bytes=48 * MIB),
        cost_estimate=cost(2 * (gw + 2) * gt * channels * tile * tile * bank, 30),
    )(index, tiles, near, far, kernels)

    count = len(received)
    rates, wall_out = pl.pallas_call(
        functools.partial(finish_kernel, (gw, gt, entries, peers, cap, walls, picks, merged)),
        name="columns_and_walls",
        out_shape=(jax.ShapeDtypeStruct((gw, gt, channels, tile), bf16), stack(walls)),
        in_specs=[HBM] + [VMEM] * (4 + count),
        out_specs=(HBM, HBM),
        scratch_shapes=[
            pltpu.SMEM((gw, LANES), i32),
            buffer(bank * 2 * depth + 1),
            buffer(wall_bank * peers * cap + 1),
            pltpu.VMEM((2, gw, channels, tile), bf16),
            buffer(walls),
            pltpu.SemaphoreType.DMA((6,)),
        ],
        compiler_params=pltpu.CompilerParams(vmem_limit_bytes=44 * MIB),
        cost_estimate=cost(2 * peers * cap * channels * tile * tile * wall_bank, 8),
    )(
        index,
        own,
        *received,
        kernels,
        wall_kernels,
        rates.reshape(gw, gt, channels, tile),
    )
    return rates, wall_out.reshape(1, 1, walls, channels, tile)


def solution(mesh):
    in_specs = (
        P("weld", "trans", None, None),
        P("weld", "trans", None),
        P("weld", "trans", None),
        P(),
        P("weld", "trans", None, None),
        P("weld", "trans", None, None),
        P("weld", "trans", None, None),
        P(),
    )
    out_specs = (P("weld", "trans", None, None), P("weld", "trans", None, None, None))
    return jax.shard_map(
        on_device, mesh=mesh, in_specs=in_specs, out_specs=out_specs, check_vma=False
    )
```

```python
import functools

import jax
import jax.numpy as jnp
from jax import lax
from jax.experimental import pallas as pl
from jax.experimental.pallas import tpu as pltpu
from jax.sharding import PartitionSpec as P

SMEM = pl.BlockSpec(memory_space=pltpu.SMEM)
VMEM = pl.BlockSpec(memory_space=pltpu.VMEM)
HBM = pl.BlockSpec(memory_space=pl.ANY)
MIB = 1 << 20
GROUPS = 2
LANES = 128
WALL_LANE = 32


def pick(cond, a, b):
    return lax.select(cond, jnp.int32(a), jnp.int32(b))


def index_kernel(dims, off_ref, kind_ref, slot_ref, wkind_ref, out_ref):
    gw, gt, bank, wall_bank, peers, cap = dims
    t = lax.axis_index("trans")
    off, kind = off_ref[...], kind_ref[...]
    dr = (off * 11) >> 5
    row = lax.broadcasted_iota(jnp.int32, off.shape, 1)
    per = gw // GROUPS
    band = lax.rem(row, per) + dr
    col = lax.broadcasted_iota(jnp.int32, off.shape, 2) + (off - 3 * dr) - 1
    left, right = col < 0, col >= gt
    side = left | right
    rows = per + 2
    local = jnp.where(side, bank * rows * gt, kind * (rows * gt) + band * gt + col)
    pack = LANES // gt
    for n in range(off.shape[0]):
        out_ref[n // pack, :, n % pack * gt : (n % pack + 1) * gt] = local[n]
    even_t = lax.rem(t, 2) == 0
    depth = gw + 2
    base = jnp.where(left, pick(even_t, depth, 0), pick(even_t, 0, depth))
    edge = (left & (t == 0)) | (right & (t == peers - 1))
    sides = jnp.where(side & ~edge, kind * (2 * depth) + base + row + dr, bank * 2 * depth)
    last = out_ref.shape[0] - 1
    for n in range(off.shape[0]):
        out_ref[last, :, 2 * n : 2 * n + 1] = sides[n, :, :1]
        out_ref[last, :, 2 * n + 1 : 2 * n + 2] = sides[n, :, gt - 1 :]
    slot = slot_ref[...]
    sender = slot // cap
    wall = jnp.where(
        slot >= peers * cap,
        wall_bank * peers * cap,
        wkind_ref[...] * (peers * cap) + (sender ^ t) * cap + (slot - sender * cap),
    )
    picks = slot.shape[1]
    for q in range(slot.shape[0] // gw):
        at = WALL_LANE + q * picks
        out_ref[last, :, at : at + picks] = wall[q * gw : (q + 1) * gw]


def blank(ref):
    ref[ref.shape[0] - 1] = jnp.zeros(ref.shape[1:], ref.dtype)


def listed(held_ref, count, list_ref, owner, out_ref):
    empty = jnp.zeros(held_ref.shape[1:], held_ref.dtype)
    for c in range(list_ref.shape[1]):
        item = list_ref[owner, c]
        tile = held_ref[jnp.minimum(item, count - 1)]
        out_ref[c] = jnp.where(item < count, tile, empty)


def first_kernel(dims, early, list_ref, x_ref, near_ref, far_ref, *refs):
    gw, gt = dims
    outs, (picks_ref, held_ref, sem) = refs[: len(early)], refs[len(early) :]
    w, t = lax.axis_index("weld"), lax.axis_index("trans")
    even = lax.rem(w, 2) == 0

    def span(first, count):
        return pl.ds(first * gt, count * gt)

    half = gw // 2
    loads = [
        pltpu.make_async_copy(list_ref, picks_ref, sem.at[0]),
        pltpu.make_async_copy(x_ref.at[span(0, half)], held_ref.at[span(0, half)], sem.at[1]),
        pltpu.make_async_copy(
            x_ref.at[span(half, half)], held_ref.at[span(half, half)], sem.at[2]
        ),
    ]
    for copy in loads:
        copy.start()
    for copy in loads:
        copy.wait()
    near_ref[...] = held_ref[span(pick(even, gw - 1, 0), 1)]
    far_ref[...] = held_ref[span(pick(even, 0, gw - 1), 1)]
    for k, ref in zip(early, outs):
        listed(held_ref, gw * gt, picks_ref, t ^ k, ref)


def second_kernel(dims, late, merged, list_ref, held_ref, near_ref, far_ref, *outs):
    gw, gt, cap = dims
    w, t = lax.axis_index("weld"), lax.axis_index("trans")
    even_w, even_t = lax.rem(w, 2) == 0, lax.rem(t, 2) == 0
    for which in range(2):
        if merged:
            ref, base = outs[late.index((1, 3)[which])], cap
        else:
            ref, base = outs[len(late) + which], 0
        column = pick(even_t, gt - 1, 0) if which == 0 else pick(even_t, 0, gt - 1)
        ref[base + pick(even_w, gw + 1, 0)] = near_ref[column]
        ref[base + pick(even_w, 0, gw + 1)] = far_ref[column]
        for r in range(gw):
            ref[base + 1 + r] = held_ref[r * gt + column]
    for k, ref in zip(late, outs):
        listed(held_ref, gw * gt, list_ref, t ^ k, ref)


def tree(terms):
    while len(terms) > 1:
        terms = [sum(terms[i : i + 2][1:], terms[i]) for i in range(0, len(terms), 2)]
    return terms[0]


def products(rows, bank_ref, j, targets):
    tiles = rows.shape[0] // 16
    both = jnp.concatenate([bank_ref[j], bank_ref[j + 1]], axis=1)
    wide = jnp.dot(rows, both, preferred_element_type=jnp.float32).astype(jnp.bfloat16)
    for h in range(2):
        part = wide[:, 128 * h : 128 * (h + 1)].reshape(tiles, 16, 128)
        for ref, step, at, low, count in targets:
            start = (j + h) * step + at
            ref[start : start + count] = part[low : low + count]


def local_kernel(dims, index_ref, x_ref, near_ref, far_ref, bank, out_ref, index, *scratch):
    gw, gt, entries = dims
    tables, sem = scratch[:-1], scratch[-1]
    pack = LANES // gt
    even = lax.rem(lax.axis_index("weld"), 2) == 0
    per, kernels = gw // GROUPS, bank.shape[0]
    step = (per + 2) * gt
    fetch = pltpu.make_async_copy(index_ref.at[: entries // pack], index, sem)
    fetch.start()
    for table in tables:
        blank(table)
    before = jnp.where(even, far_ref[...], near_ref[...])
    after = jnp.where(even, near_ref[...], far_ref[...])

    def gather(table, r, c):
        terms = [
            table[index[n // pack, r, n % pack * gt + c]].astype(jnp.float32)
            for n in range(entries)
        ]
        out_ref[r * gt + c] = tree(terms).astype(out_ref.dtype)

    share = per * gt * 2 // kernels
    for g, table in enumerate(tables):
        low, high = (0 if g == 0 else g * per + 2), g * per + per + 2
        parts = [before] if low == 0 else []
        parts.append(x_ref[max(low - 1, 0) * gt : min(high - 1, gw) * gt])
        if high == gw + 2:
            parts.append(after)
        rows = jnp.concatenate(parts, axis=0) if len(parts) > 1 else parts[0]
        fresh = (high - low) * gt
        targets = [(table, step, step - fresh, 0, fresh)]
        if g + 1 < GROUPS:
            targets.append((tables[g + 1], step, 0, fresh - 2 * gt, 2 * gt))
        cells = [((g - 1) * per + i // gt, i % gt) for i in range(per * gt)] if g else []
        for j in range(0, kernels, 2):
            products(rows.reshape(fresh * 16, 128), bank, j, targets)
            for r, c in cells[j // 2 * share : (j // 2 + 1) * share]:
                gather(tables[g - 1], r, c)
        if g == 0:
            fetch.wait()
    for r in range(gw - per, gw):
        for c in range(gt):
            gather(tables[-1], r, c)


def finish_kernel(dims, index_ref, *refs):
    gw, gt, entries, peers, cap, walls, picks, merged = dims
    own_ref = refs[0]
    count = peers - 1 + (0 if merged else 2)
    got = refs[1 : 1 + count]
    got = got[: peers - 1][::-1] + got[peers - 1 :]
    bank_ref, wall_bank_ref, local_ref, rates_ref, walls_ref = refs[1 + count : 6 + count]
    index, table_ref, wall_table_ref, cols_ref, done_ref, sem = refs[6 + count :]
    fetch = pltpu.make_async_copy(index_ref.at[index_ref.shape[0] - 1], index, sem.at[0])
    inner = pltpu.make_async_copy(
        local_ref.at[:, 1 : gt - 1], rates_ref.at[:, 1 : gt - 1], sem.at[1]
    )
    edges = [
        pltpu.make_async_copy(cols_ref.at[e], rates_ref.at[:, c], sem.at[2 + e])
        for e, c in enumerate((0, gt - 1))
    ]
    part = walls // 2
    ready = [
        pltpu.make_async_copy(
            done_ref.at[pl.ds(h * part, part)], walls_ref.at[pl.ds(h * part, part)], sem.at[4 + h]
        )
        for h in range(2)
    ]
    fetch.start()
    inner.start()
    depth = gw + 2
    if merged:
        sides = [got[0][cap : cap + depth], got[2][cap : cap + depth]]
    else:
        sides = [got[-2][...], got[-1][...]]
    blank(table_ref)
    blank(wall_table_ref)
    slots = peers * cap
    received = jnp.concatenate([own_ref[...]] + [g[:cap] for g in got[: peers - 1]], axis=0)
    received = received.reshape(slots * 16, 128)
    for j in range(0, wall_bank_ref.shape[0], 2):
        products(received, wall_bank_ref, j, [(wall_table_ref, slots, 0, 0, slots)])
    ring = jnp.concatenate(sides, axis=0).reshape(2 * depth * 16, 128)
    for j in range(0, bank_ref.shape[0], 2):
        products(ring, bank_ref, j, [(table_ref, 2 * depth, 0, 0, 2 * depth)])
    fetch.wait()
    for e, c in enumerate((0, gt - 1)):
        for r in range(gw):
            terms = [table_ref[index[r, 2 * n + e]].astype(jnp.float32) for n in range(entries)]
            base = local_ref[r, c].astype(jnp.float32)
            cols_ref[e, r] = (base + tree(terms)).astype(cols_ref.dtype)
        edges[e].start()
    for j in range(walls):
        lane = WALL_LANE + j // gw * picks
        picked = [
            wall_table_ref[index[j % gw, lane + m]].astype(jnp.float32) for m in range(picks)
        ]
        sums = tree(picked)
        done_ref[j] = (sums / (1.0 + sums[0:1, :])).astype(done_ref.dtype)
        if (j + 1) % part == 0:
            ready[j // part].start()
    for copy in (inner, *edges, *ready):
        copy.wait()


def pairing(count, shift):
    pairs = []
    for low in range(shift, count - 1, 2):
        pairs += [(low, low + 1), (low + 1, low)]
    return pairs


def on_device(
    features, pair_offsets, pair_kernel, kernels, send_list, wall_slots, wall_kernel, wall_kernels
):
    gw, gt, channels, tile = features.shape
    entries = pair_offsets.shape[2]
    bank, wall_bank = kernels.shape[0], wall_kernels.shape[0]
    peers, cap = send_list.shape[2:]
    walls, picks = wall_slots.shape[2:]
    weld = lax.axis_size("weld")
    merged = peers == 4
    depth = gw + 2
    i32, bf16 = jnp.int32, jnp.bfloat16
    total = gw * gt
    tiles = features.reshape(total, channels, tile)
    lists = send_list.reshape(peers, cap)

    def stack(n):
        return jax.ShapeDtypeStruct((n, channels, tile), bf16)

    def buffer(n):
        return pltpu.VMEM((n, channels, tile), bf16)

    def cost(flops, mib):
        return pl.CostEstimate(flops=flops, bytes_accessed=mib * MIB, transcendentals=0)

    early = (2,) if merged else tuple(range(2, peers))
    late = (1, 3, 0) if merged else (1, 0)
    near_out, far_out, *early_out = pl.pallas_call(
        functools.partial(first_kernel, (gw, gt), early),
        name="edge_rows",
        out_shape=(stack(gt), stack(gt)) + (stack(cap),) * len(early),
        in_specs=[HBM, HBM],
        out_specs=(VMEM,) * (2 + len(early)),
        scratch_shapes=[
            pltpu.SMEM((peers, cap), i32),
            buffer(total),
            pltpu.SemaphoreType.DMA((3,)),
        ],
        compiler_params=pltpu.CompilerParams(vmem_limit_bytes=56 * MIB),
        cost_estimate=cost(0, 2),
    )(lists, tiles)
    near = lax.ppermute(near_out, "weld", pairing(weld, 0))
    far = lax.ppermute(far_out, "weld", pairing(weld, 1))
    got = {}
    for k, message in zip(early, early_out):
        got[k] = lax.ppermute(message, "trans", [(i, i ^ k) for i in range(peers)])

    planes = entries * gt // LANES + 1
    index = pl.pallas_call(
        functools.partial(index_kernel, (gw, gt, bank, wall_bank, peers, cap)),
        name="pair_index",
        out_shape=jax.ShapeDtypeStruct((planes, gw, LANES), i32),
        in_specs=[VMEM] * 4,
        out_specs=VMEM,
        cost_estimate=cost(1_000_000, 3),
    )(
        pair_offsets.transpose(2, 0, 1),
        pair_kernel.transpose(2, 0, 1),
        wall_slots.reshape(walls, picks),
        wall_kernel.reshape(walls, picks),
    )

    lengths = [cap + (depth if merged and k else 0) for k in late]
    if not merged:
        lengths += [depth, depth]
    late_out = pl.pallas_call(
        functools.partial(second_kernel, (gw, gt, cap), late, merged),
        name="edge_columns",
        out_shape=tuple(stack(n) for n in lengths),
        in_specs=[SMEM, VMEM, VMEM, VMEM],
        out_specs=(VMEM,) * len(lengths),
        compiler_params=pltpu.CompilerParams(vmem_limit_bytes=8 * MIB),
        cost_estimate=cost(0, 2),
    )(lists, tiles, near, far)
    for k, message in zip(late, late_out):
        if k:
            got[k] = lax.ppermute(message, "trans", [(i, i ^ k) for i in range(peers)])
    own = late_out[late.index(0)]
    received = [got[k] for k in range(peers - 1, 0, -1)]
    if not merged:
        received += [
            lax.ppermute(late_out[len(late) + s], "trans", pairing(peers, s)) for s in range(2)
        ]

    step = (gw // GROUPS + 2) * gt
    rates = pl.pallas_call(
        functools.partial(local_kernel, (gw, gt, entries)),
        name="local_pairs",
        out_shape=stack(total),
        in_specs=[HBM] + [VMEM] * 4,
        out_specs=VMEM,
        scratch_shapes=[
            pltpu.SMEM((planes - 1, gw, LANES), i32),
            *[buffer(bank * step + 1)] * GROUPS,
            pltpu.SemaphoreType.DMA,
        ],
        compiler_params=pltpu.CompilerParams(vmem_limit_bytes=48 * MIB),
        cost_estimate=cost(2 * (gw + 2) * gt * channels * tile * tile * bank, 30),
    )(index, tiles, near, far, kernels)

    count = len(received)
    rates, wall_out = pl.pallas_call(
        functools.partial(finish_kernel, (gw, gt, entries, peers, cap, walls, picks, merged)),
        name="columns_and_walls",
        out_shape=(jax.ShapeDtypeStruct((gw, gt, channels, tile), bf16), stack(walls)),
        in_specs=[HBM] + [VMEM] * (4 + count),
        out_specs=(HBM, HBM),
        scratch_shapes=[
            pltpu.SMEM((gw, LANES), i32),
            buffer(bank * 2 * depth + 1),
            buffer(wall_bank * peers * cap + 1),
            pltpu.VMEM((2, gw, channels, tile), bf16),
            buffer(walls),
            pltpu.SemaphoreType.DMA((6,)),
        ],
        compiler_params=pltpu.CompilerParams(vmem_limit_bytes=44 * MIB),
        cost_estimate=cost(2 * peers * cap * channels * tile * tile * wall_bank, 8),
    )(
        index,
        own,
        *received,
        kernels,
        wall_kernels,
        rates.reshape(gw, gt, channels, tile),
    )
    return rates, wall_out.reshape(1, 1, walls, channels, tile)


def solution(mesh):
    in_specs = (
        P("weld", "trans", None, None),
        P("weld", "trans", None),
        P("weld", "trans", None),
        P(),
        P("weld", "trans", None, None),
        P("weld", "trans", None, None),
        P("weld", "trans", None, None),
        P(),
    )
    out_specs = (P("weld", "trans", None, None), P("weld", "trans", None, None, None))
    return jax.shard_map(
        on_device, mesh=mesh, in_specs=in_specs, out_specs=out_specs, check_vma=False
    )
```
